32 devices in a mesh: row: 4 (over x, core), col: 8 (over z, y).
Axes of the slice: x: 2, y: 2, z: 4, core: 2. Of those that a mesh axis runs over, the one named last changes fastest.
Arguments:
- corner: bfloat16 [25600, 25600], P('row', 'col'), may hold values from -32 to 32
- edge: bfloat16 [25600, 25600], P('row', 'col'), may hold values from -32 to 32
- sketch: bfloat16 [25600, 448], P('col'), may hold values from -6 to 6
Outputs:
- corner_new: float32 [400, 400], replicated
- edge_new: float32 [400, 400], replicated
The draws below stay inside these ranges and needn't reach their ends.
All inputs are finite; a program needn't handle non-finite values.
Results may differ from the reference program's by a relative error of at most 0.0015.
Values may be sent and summed in bfloat16 or wider, within the bound.
A program may use at most 256 MiB of HBM per device.

```python
import math
import jax
import jax.numpy as jnp
from jax import lax

CHI = 400
DD = 64
SKETCH = 448
RANK = 400
ORDER = 25600
N_ROW = 4


def dominant(key, shift, spread):
    order = CHI * DD
    noise = jax.random.normal(jax.random.fold_in(key, 23), (order, order), jnp.float32)
    matrix = shift * jnp.eye(order, dtype=jnp.float32) + spread / math.sqrt(order) * noise
    return matrix.astype(jnp.bfloat16)


def draw_corner(key, part):
    return dominant(jax.random.fold_in(key, 101), 3.0, 2.0)


def draw_edge(key, part):
    return dominant(jax.random.fold_in(key, 202), 2.0, 2.0)


def levels(own_key, shape, pieces, smallest, largest):
    def one(axis_at, shards_of):
        draws = jax.random.uniform(jax.random.fold_in(jax.random.fold_in(own_key, 6), axis_at), (shards_of,), jnp.float32, smallest / len(pieces), largest / len(pieces))
        return jnp.repeat(jnp.exp(draws), shape[axis_at] // shards_of).reshape((-1,) + (1,) * (len(shape) - axis_at - 1))

    loudness = one(*pieces[0])
    for cut in pieces[1:]:
        loudness = loudness * one(*cut)
    return loudness


def bell_draw(rng, extent, scale, reach, split=(), held_as=jnp.bfloat16):
    level = levels(rng, extent, split, -0.22, 0.18) if split else 1.0
    values = jax.random.normal(rng, extent, jnp.float32) * scale * level
    return jnp.minimum(jnp.maximum(values, -reach), reach).astype(held_as)


def setup_inputs(seed: int = 0) -> dict:
    streams_of = jax.random.split(jax.random.key(seed), 4)
    return {
        "corner": draw_corner(jax.random.fold_in(streams_of[3], 71), 0),
        "edge": draw_edge(jax.random.fold_in(streams_of[3], 71), 0),
        "sketch": bell_draw(streams_of[2], (ORDER, SKETCH), 1.0, 6.0, ((0, 8),)),
    }


def apply_blocks(matrix, right):
    blocks = matrix.reshape(N_ROW, ORDER // N_ROW, ORDER)
    result = lax.map(lambda block: jnp.dot(block.astype(jnp.float32), right.astype(jnp.float32), preferred_element_type=jnp.float32), blocks)
    return result.reshape(ORDER, right.shape[1])

def reference(corner, edge, sketch):
    sampled = apply_blocks(corner, sketch)
    gram = jnp.dot(sampled.T, sampled, precision=lax.Precision.HIGHEST)
    lower = jnp.linalg.cholesky(gram)
    basis = lax.linalg.triangular_solve(lower, sampled, left_side=False, lower=True, transpose_a=True)
    projector = basis[:, SKETCH - RANK:].astype(jnp.bfloat16)
    wide = projector.astype(jnp.float32)
    corner_image = apply_blocks(corner, projector)
    edge_image = apply_blocks(edge, projector)
    corner_new = jnp.dot(wide.T, corner_image, precision=lax.Precision.HIGHEST)
    edge_new = jnp.dot(wide.T, edge_image, precision=lax.Precision.HIGHEST)
    return (corner_new, edge_new)
```

```python
import functools

import jax
import jax.numpy as jnp
from jax import lax
from jax.experimental import pallas as pl
from jax.experimental.pallas import tpu as pltpu
from jax.sharding import PartitionSpec as P

RANK = 400
HIGHEST = lax.Precision.HIGHEST
BLOCK = 128
TILE = 8
LANES = 128
SLOTS = 3
AHEAD = 2
VMEM_LIMIT = 67043328


def across(left, right):
    return lax.dot_general(left, right, (((1,), (1,)), ((), ())), preferred_element_type=jnp.float32)


def plan(part, n_row):
    sub = LANES if part % LANES == 0 else part
    pieces = part // sub
    if pieces % 5 or pieces < 25:
        return sub, pieces, 1, [pieces], pieces, [pieces - 1 + n_row], 0, 1
    groups = []
    while sum(groups) + 12 < pieces:
        groups.append(6)
    left = pieces - sum(groups)
    groups += [left - left // 2 + left % 2, left // 2 - left % 2] if left > 6 else [left]
    lead = sum(groups[:2])
    lag, stride = 3, 8
    total = pieces + lag + stride * (n_row - 1) - lead
    parts = [5, 5]
    total -= 10
    for g in range(2, len(groups)):
        parts.append(total // (len(groups) - g))
        total -= parts[-1]
    return sub, pieces, 5, groups, lead, parts, lag, stride


def move_kernel(n_row, n_col, shape, corner, edge, sketch, corner_out, edge_out, cols, ring, images, mine, away, near, upper, lower, staged, rows, tmp, *sems):
    (load_sem, near_send, near_recv, chain_send, upper_recv, lower_recv,
     cast_send, cast_recv, back_send, back_recv, swap_send, swap_recv) = sems
    sub, pieces, tiles, groups, lead, parts, lag, stride = shape
    ratio = n_col // n_row
    me_row, me_col = lax.axis_index("row"), lax.axis_index("col")
    place, half = me_col // ratio, lax.rem(me_col, ratio)
    part = cols.shape[1]
    chunk = part // tiles
    per_tile = pieces // tiles

    owner = place == me_row
    has_upper = jnp.logical_and(place >= me_row, place < n_row - 1)
    has_lower = jnp.logical_and(place <= me_row, place > 0)
    to_lower, to_upper = place > me_row, place < me_row
    back_up = jnp.logical_and(place >= me_row, place < n_row - 1)
    back_down = jnp.logical_and(place <= me_row, place > 0)

    def partner(d):
        return (me_row, place * ratio + lax.rem(half + d, ratio))

    def peer(d):
        return (lax.rem(me_row + d, n_row), me_col)

    up_id = (me_row, lax.rem(me_col + ratio, n_col))
    down_id = (me_row, lax.rem(me_col + n_col - ratio, n_col))

    def remote(source, target, send, recv, device):
        return pltpu.make_async_remote_copy(
            src_ref=source, dst_ref=target, send_sem=send, recv_sem=recv,
            device_id=device, device_id_type=pl.DeviceIdType.MESH,
        )

    def span(s, count=1):
        if pieces == 1:
            return pl.ds(0, sub)
        return pl.ds(pl.multiple_of(s * sub, sub), count * sub)

    def near_copy(d, s):
        return remote(away.at[d - 1, :, span(s)], near.at[d - 1, :, span(s)],
                      near_send.at[d - 1, s], near_recv.at[d - 1, s], partner(d))

    def down_copy(s):
        return remote(staged.at[:, span(s)], upper.at[:, span(s)], chain_send.at[s], upper_recv.at[s], down_id)

    def up_copy(s):
        return remote(staged.at[:, span(s)], lower.at[:, span(s)], chain_send.at[s], lower_recv.at[s], up_id)

    def cast_copy(d, s):
        return remote(rows.at[0, :, span(s)], cols.at[:, span(s)], cast_send.at[d - 1, s], cast_recv.at[s], peer(d))

    def back_copy(way, s):
        return remote(rows.at[0, :, span(s)], rows.at[0, :, span(s)], back_send.at[way, s], back_recv.at[s],
                      up_id if way else down_id)

    def swap_copy(d, s):
        return remote(rows.at[0, :, span(s)], rows.at[ratio - d, :, span(s)],
                      swap_send.at[d - 1, s], swap_recv.at[ratio - d - 1, s], partner(d))

    starts = [sum(groups[:g]) for g in range(len(groups))]

    def load(matrix, t, g, slot):
        k0, width = starts[g] * sub, groups[g] * sub
        copies = []
        for pos in range(ratio):
            at = pl.multiple_of(lax.rem(half + pos, ratio) * part + t * chunk, TILE * 2)
            copies.append(pltpu.make_async_copy(
                matrix.at[pl.ds(at, chunk), k0 : k0 + width], ring.at[slot, pos, :, 0:width], load_sem.at[slot, pos]))
        return copies

    def product(left, t, g, slot):
        k0, width = starts[g] * sub, groups[g] * sub
        operand = left[:, k0 : k0 + width]
        if chunk % LANES == 0:
            block = ring[slot, :, :, 0:width].reshape(ratio * chunk, width)
            found = across(operand, block)
            return [found[:, p * chunk : (p + 1) * chunk] for p in range(ratio)]
        return [across(operand, ring[slot, p, :, 0:width]) for p in range(ratio)]

    barrier = pltpu.get_barrier_semaphore()

    def greet(device):
        pl.semaphore_signal(barrier, inc=1, device_id=device, device_id_type=pl.DeviceIdType.MESH)

    n_groups = len(groups)
    steps = [("sample", g) for g in range(n_groups)]

    def start_sample(t, g, slot):
        for copy in load(corner, t, g, slot):
            copy.start()

    def start_image(m, t, g, slot):
        for copy in load(edge if m else corner, t, g, slot):
            copy.start()

    total_sample = tiles * n_groups

    def start_at(index):
        if index < total_sample:
            start_sample(index // n_groups, index % n_groups, index % SLOTS)
        else:
            index -= total_sample
            g, rest = divmod(index, 2 * tiles)
            start_image(rest % 2, rest // 2, g, (index + total_sample) % SLOTS)

    for index in range(AHEAD):
        start_at(index)
    for d in range(1, ratio):
        greet(partner(d))
    for d in range(1, n_row):
        greet(peer(d))

    @pl.when(place < n_row - 1)
    def _():
        greet(up_id)

    @pl.when(place > 0)
    def _():
        greet(down_id)

    ends = (place < n_row - 1).astype(jnp.int32) + (place > 0).astype(jnp.int32)
    pl.semaphore_wait(barrier, ratio - 1 + n_row - 1 + ends)

    def gather(s):
        total = mine[:, span(s)].astype(jnp.float32)
        for d in range(1, ratio):
            near_copy(d, s).wait_recv()
            total += near[d - 1, :, span(s)].astype(jnp.float32)
        tmp[...] = total

        @pl.when(has_upper)
        def _():
            down_copy(s).wait_recv()
            tmp[...] += upper[:, span(s)].astype(jnp.float32)

        @pl.when(has_lower)
        def _():
            up_copy(s).wait_recv()
            tmp[...] += lower[:, span(s)].astype(jnp.float32)

        @pl.when(owner)
        def _():
            value = tmp[...].astype(jnp.bfloat16)
            rows[0, :, span(s)] = value
            cols[:, span(s)] = value
            for d in range(1, n_row):
                cast_copy(d, s).start()

            @pl.when(place < n_row - 1)
            def _():
                back_copy(1, s).start()

            @pl.when(place > 0)
            def _():
                back_copy(0, s).start()

        @pl.when(to_lower)
        def _():
            staged[:, span(s)] = tmp[...].astype(jnp.bfloat16)
            down_copy(s).start()

        @pl.when(to_upper)
        def _():
            staged[:, span(s)] = tmp[...].astype(jnp.bfloat16)
            up_copy(s).start()

    def hand_back(s):
        @pl.when(jnp.logical_not(owner))
        def _():
            back_copy(0, s).wait_recv()

            @pl.when(jnp.logical_and(to_lower, place < n_row - 1))
            def _():
                back_copy(1, s).start()

            @pl.when(jnp.logical_and(to_upper, place > 0))
            def _():
                back_copy(0, s).start()

        for d in range(1, ratio):
            swap_copy(d, s).start()

    wait = lag + stride * jnp.abs(place - me_row)

    def advance(first, p):
        if first < pieces:
            @pl.when(p < pieces)
            def _():
                gather(p)

        @pl.when(jnp.logical_and(p >= wait, p < wait + pieces))
        def _():
            hand_back(p - wait)

    def positions(first, count):
        def one(i, carry):
            advance(first, first + i)
            return carry

        lax.fori_loop(0, count, one, 0)

    early = [0] * tiles
    if tiles > 1:
        early = [0, 0, 2, 2, 3]

    def sample_tile(t, carry):
        for g in range(n_groups):
            index = t * n_groups + g
            slot = lax.rem(index, SLOTS)
            for copy in load(corner, t, g, slot):
                copy.wait()
            later = g + AHEAD
            if later < n_groups:
                start_sample(t, later, lax.rem(index + AHEAD, SLOTS))
            else:
                later_t, later_g = t + later // n_groups, later % n_groups

                @pl.when(later_t < tiles)
                def _():
                    start_sample(later_t, later_g, lax.rem(index + AHEAD, SLOTS))

            found = product(sketch, t, g, slot)
            if g > 0:
                found = [images[0, 0, p] + found[p] for p in range(ratio)]
            if g < n_groups - 1:
                for p in range(ratio):
                    images[0, 0, p] = found[p]
            else:
                at = span(t * per_tile, per_tile)
                mine[:, at] = found[0].astype(jnp.bfloat16)
                for d in range(1, ratio):
                    away[d - 1, :, at] = found[d].astype(jnp.bfloat16)
        for d in range(1, ratio):
            for i in range(per_tile):
                near_copy(d, t * per_tile + i).start()
        if tiles > 1:
            before = jnp.where(t > 2, (t - 2) * 2, 0)
            count = jnp.where(t < 2, 0, jnp.where(t == 4, 3, 2))

            def one(i, inner):
                advance(0, before + i)
                return inner

            lax.fori_loop(0, count, one, 0)
        return carry

    lax.fori_loop(0, tiles, sample_tile, 0)
    done = sum(early)
    for index in range(AHEAD):
        start_at(total_sample + index)
    positions(done, lead - done)

    first = lead
    for g in range(n_groups):
        for i in range(groups[g]):
            s = starts[g] + i

            @pl.when(jnp.logical_not(owner))
            def _():
                cast_copy(1, s).wait_recv()

        every = parts[g] // tiles

        def image_tile(t, carry):
            for m in range(2):
                index = total_sample + (g * tiles + t) * 2 + m
                slot = lax.rem(index, SLOTS)
                for copy in load(edge if m else corner, t, g, slot):
                    copy.wait()
                ahead = t * 2 + m + AHEAD
                into = lax.rem(index + AHEAD, SLOTS)

                @pl.when(ahead < 2 * tiles)
                def _():
                    start_image(m, t + 1, g, into)

                if g + 1 < n_groups:
                    @pl.when(ahead >= 2 * tiles)
                    def _():
                        start_image(m, 0, g + 1, into)

                found = product(cols, t, g, slot)
                for p in range(ratio):
                    if g == 0:
                        images[m, t, p] = found[p]
                    else:
                        images[m, t, p] += found[p]
            for i in range(every):
                advance(first, first + t * every + i)
            return carry

        lax.fori_loop(0, tiles, image_tile, 0)
        tail = parts[g] - every * tiles
        if tail:
            positions(first + every * tiles, tail)
        first += parts[g]

    corner_out[...] = jnp.zeros_like(corner_out)
    edge_out[...] = jnp.zeros_like(edge_out)

    def left_tile(t, carry):
        for d in range(1, ratio):
            for i in range(per_tile):
                swap_copy(d, t * per_tile + i).wait_recv()
        at = span(t * per_tile, per_tile)
        for m, out in ((0, corner_out), (1, edge_out)):
            if chunk % LANES == 0:
                left = jnp.concatenate([rows[p, :, at] for p in range(ratio)], axis=1)
                right = jnp.concatenate([images[m, t, p].astype(jnp.bfloat16) for p in range(ratio)], axis=1)
                out[...] += across(left, right)
            else:
                for p in range(ratio):
                    out[...] += across(rows[p, :, at], images[m, t, p].astype(jnp.bfloat16))
        return carry

    lax.fori_loop(0, tiles, left_tile, 0)

    def finish(s, carry):
        for d in range(1, ratio):
            near_copy(d, s).wait_send()
            swap_copy(d, s).wait_send()

        @pl.when(owner)
        def _():
            for d in range(1, n_row):
                cast_copy(d, s).wait_send()

        @pl.when(jnp.logical_not(owner))
        def _():
            down_copy(s).wait_send()

        @pl.when(back_up)
        def _():
            back_copy(1, s).wait_send()

        @pl.when(back_down)
        def _():
            back_copy(0, s).wait_send()

        return carry

    lax.fori_loop(0, pieces, finish, 0)


def move(corner, edge, sketch):
    n_row, n_col = lax.axis_size("row"), lax.axis_size("col")
    height, part = corner.shape
    width = sketch.shape[0]
    ratio = n_col // n_row
    assert ratio * n_row == n_col and height == ratio * part
    shape = plan(part, n_row)
    sub, pieces, tiles, groups = shape[:4]
    chunk = part // tiles
    dma = pltpu.SemaphoreType.DMA
    half = jnp.bfloat16
    square = jax.ShapeDtypeStruct((width, width), jnp.float32)
    vmem = pl.BlockSpec(memory_space=pltpu.VMEM)
    hbm = pl.BlockSpec(memory_space=pl.ANY)
    return pl.pallas_call(
        functools.partial(move_kernel, n_row, n_col, shape),
        out_shape=(square, square, jax.ShapeDtypeStruct((width, part), half)),
        in_specs=[hbm, hbm, vmem],
        out_specs=(vmem, vmem, vmem),
        scratch_shapes=[
            pltpu.VMEM((SLOTS, ratio, chunk, max(groups) * sub), half),
            pltpu.VMEM((2, tiles, ratio, width, chunk), jnp.float32),
            pltpu.VMEM((width, part), half),
            pltpu.VMEM((ratio - 1, width, part), half),
            pltpu.VMEM((ratio - 1, width, part), half),
            pltpu.VMEM((width, part), half),
            pltpu.VMEM((width, part), half),
            pltpu.VMEM((width, part), half),
            pltpu.VMEM((ratio, width, part), half),
            pltpu.VMEM((width, sub), jnp.float32),
            dma((SLOTS, ratio)),
            dma((ratio - 1, pieces)), dma((ratio - 1, pieces)),
            dma((pieces,)), dma((pieces,)), dma((pieces,)),
            dma((n_row - 1, pieces)), dma((pieces,)),
            dma((2, pieces)), dma((pieces,)),
            dma((ratio - 1, pieces)), dma((ratio - 1, pieces)),
        ],
        compiler_params=pltpu.CompilerParams(
            collective_id=2, has_side_effects=True, vmem_limit_bytes=VMEM_LIMIT),
    )(corner, edge, sketch)


def eliminate(block):
    count = block.shape[0] // TILE
    row_ids = lax.broadcasted_iota(jnp.int32, (TILE, BLOCK), 0)
    lane_ids = lax.broadcasted_iota(jnp.int32, (TILE, BLOCK), 1)
    work = [block[t * TILE : (t + 1) * TILE, :] for t in range(count)]
    other = [(lane_ids == row_ids + t * TILE).astype(jnp.float32) for t in range(count)]
    for step in range(count * TILE):
        home, place = divmod(step, TILE)
        column = [jnp.broadcast_to(work[t][:, step : step + 1], (TILE, BLOCK)) for t in range(home, count)]
        scale = 1.0 / column[0][place : place + 1, :]
        pivot_row = work[home][place : place + 1, :] * scale
        other_row = other[home][place : place + 1, :] * scale
        for t in range(home, count):
            factor = column[t - home]
            if t == home:
                factor = jnp.where(row_ids > place, factor, 0.0)
            work[t] = work[t] - factor * pivot_row
            other[t] = other[t] - factor * other_row
    done = []
    for t in range(count):
        diagonal = jnp.sum(jnp.where(lane_ids == row_ids + t * TILE, work[t], 0.0), axis=1, keepdims=True)
        done.append(other[t] / jnp.sqrt(diagonal))
    return jnp.concatenate(done, axis=0)


def factor_kernel(gram, out, held):
    size = gram.shape[0]
    padded = held.shape[0]
    ids_r = lax.broadcasted_iota(jnp.int32, (padded, padded), 0)
    ids_c = lax.broadcasted_iota(jnp.int32, (padded, padded), 1)
    unit = (ids_r == ids_c).astype(jnp.float32)
    held[:, :padded] = unit
    held[:, padded:] = unit
    held[:size, :size] = gram[...]
    blocks = padded // BLOCK

    def one(k, carry):
        at = pl.multiple_of(k * BLOCK, BLOCK)
        inverse = eliminate(held[pl.ds(at, BLOCK), pl.ds(at, BLOCK)])
        strip = jnp.dot(inverse, held[pl.ds(at, BLOCK), :], precision=HIGHEST, preferred_element_type=jnp.float32)
        held[pl.ds(at, BLOCK), :] = strip

        def trail(i, inner):
            low = pl.multiple_of(i * BLOCK, BLOCK)
            side = held[pl.ds(at, BLOCK), pl.ds(low, BLOCK)]
            held[pl.ds(low, BLOCK), :] -= jnp.dot(
                side.T, held[pl.ds(at, BLOCK), :], precision=HIGHEST, preferred_element_type=jnp.float32
            )
            return inner

        lax.fori_loop(k + 1, blocks, trail, 0)
        return carry

    lax.fori_loop(0, blocks, one, 0)
    out[...] = held[:size, padded : padded + size]


def inverse_factor(gram):
    size = gram.shape[0]
    padded = -(-size // BLOCK) * BLOCK
    whole = pl.pallas_call(
        factor_kernel,
        out_shape=jax.ShapeDtypeStruct((size, size), jnp.float32),
        in_specs=[pl.BlockSpec(memory_space=pltpu.VMEM)],
        out_specs=pl.BlockSpec(memory_space=pltpu.VMEM),
        scratch_shapes=[pltpu.VMEM((padded, 2 * padded), jnp.float32)],
        cost_estimate=pl.CostEstimate(
            flops=100 * padded * padded * padded, bytes_accessed=8 * size * size, transcendentals=0
        ),
    )(gram)
    return whole[size - RANK :]


def reduce_kernel(n_row, n_col, x, out, row_land, col_land, part, total, *sems):
    send_a, recv_a, send_b, recv_b, send_c, recv_c, send_d, recv_d = sems
    me_row, me_col = lax.axis_index("row"), lax.axis_index("col")
    big = x.shape[0] // n_row
    small = big // n_col

    def peer(me, shift, count):
        return lax.rem(me + shift, count)

    def row_of(shift):
        return (peer(me_row, shift, n_row), me_col)

    def col_of(shift):
        return (me_row, peer(me_col, shift, n_col))

    def copy(source, target, send, recv, device):
        return pltpu.make_async_remote_copy(
            src_ref=source, dst_ref=target, send_sem=send, recv_sem=recv,
            device_id=device, device_id_type=pl.DeviceIdType.MESH,
        )

    def at(index, size):
        return pl.ds(pl.multiple_of(index * size, TILE), size)

    barrier = pltpu.get_barrier_semaphore()
    for d in range(1, n_row):
        pl.semaphore_signal(barrier, inc=1, device_id=row_of(d), device_id_type=pl.DeviceIdType.MESH)
    for d in range(1, n_col):
        pl.semaphore_signal(barrier, inc=1, device_id=col_of(d), device_id_type=pl.DeviceIdType.MESH)
    pl.semaphore_wait(barrier, n_row + n_col - 2)

    first = []
    for d in range(1, n_row):
        chunk = x.at[at(peer(me_row, d, n_row), big), :]
        first.append(copy(chunk, row_land.at[d - 1], send_a.at[d - 1], recv_a.at[d - 1], row_of(d)))
        first[-1].start()
    summed = x[at(me_row, big), :]
    for d in range(1, n_row):
        first[d - 1].wait_recv()
        summed += row_land[d - 1]
    part[...] = summed

    second = []
    for d in range(1, n_col):
        chunk = part.at[at(peer(me_col, d, n_col), small), :]
        second.append(copy(chunk, col_land.at[d - 1], send_b.at[d - 1], recv_b.at[d - 1], col_of(d)))
        second[-1].start()
    summed = part[at(me_col, small), :]
    for d in range(1, n_col):
        second[d - 1].wait_recv()
        summed += col_land[d - 1]
    total[...] = summed

    mine = pl.ds(pl.multiple_of(me_row * big + me_col * small, TILE), small)
    third = []
    for d in range(1, n_col):
        third.append(copy(total, out.at[mine, :], send_c.at[d - 1], recv_c.at[d - 1], col_of(d)))
        third[-1].start()
    out[mine, :] = summed
    for d in range(1, n_col):
        third[d - 1].wait_recv()

    fourth = []
    for d in range(1, n_row):
        chunk = out.at[at(me_row, big), :]
        fourth.append(copy(chunk, chunk, send_d.at[d - 1], recv_d.at[d - 1], row_of(d)))
        fourth[-1].start()
    for d in range(1, n_row):
        fourth[d - 1].wait_recv()
    for sent in first + second + third + fourth:
        sent.wait_send()


def reduce_all(value, collective_id):
    n_row, n_col = lax.axis_size("row"), lax.axis_size("col")
    height, width = value.shape
    grain = n_row * n_col * TILE
    padded = -(-height // grain) * grain
    value = jnp.pad(value, ((0, padded - height), (0, 0)))
    big = padded // n_row
    small = big // n_col
    dma = pltpu.SemaphoreType.DMA
    result = pl.pallas_call(
        functools.partial(reduce_kernel, n_row, n_col),
        out_shape=jax.ShapeDtypeStruct((padded, width), jnp.float32),
        in_specs=[pl.BlockSpec(memory_space=pltpu.VMEM)],
        out_specs=pl.BlockSpec(memory_space=pltpu.VMEM),
        scratch_shapes=[
            pltpu.VMEM((n_row - 1, big, width), jnp.float32),
            pltpu.VMEM((n_col - 1, small, width), jnp.float32),
            pltpu.VMEM((big, width), jnp.float32),
            pltpu.VMEM((small, width), jnp.float32),
        ]
        + [dma((n_row - 1,)), dma((n_row - 1,)), dma((n_col - 1,)), dma((n_col - 1,))]
        + [dma((n_col - 1,)), dma((n_col - 1,)), dma((n_row - 1,)), dma((n_row - 1,))],
        compiler_params=pltpu.CompilerParams(collective_id=collective_id, has_side_effects=True),
    )(value)
    return result[:height]


def body(corner, edge, sketch):
    n_row = lax.axis_size("row")
    corner_sum, edge_sum, cols = move(corner, edge, sketch.T)
    gram = reduce_all(across(cols, cols) * (1.0 / n_row), 0)
    inverse = inverse_factor(gram)

    def renormalize(total):
        half = jnp.dot(inverse, total, precision=HIGHEST)
        return lax.dot_general(half, inverse, (((1,), (1,)), ((), ())), precision=HIGHEST)

    stacked = jnp.concatenate([renormalize(corner_sum), renormalize(edge_sum)], axis=0)
    result = reduce_all(stacked, 1)
    return result[:RANK], result[RANK:]


def solution(mesh):
    placed = (P("row", "col"), P("row", "col"), P("col", None))
    return jax.shard_map(body, mesh=mesh, in_specs=placed, out_specs=(P(), P()), check_vma=False)
```

```python
import functools

import jax
import jax.numpy as jnp
from jax import lax
from jax.experimental import pallas as pl
from jax.experimental.pallas import tpu as pltpu
from jax.sharding import PartitionSpec as P

RANK = 400
HIGHEST = lax.Precision.HIGHEST
BLOCK = 128
TILE = 8
LANES = 128
SLOTS = 3
AHEAD = 2
VMEM_LIMIT = 67043328


def across(left, right):
    return lax.dot_general(left, right, (((1,), (1,)), ((), ())), preferred_element_type=jnp.float32)


def plan(part, n_row):
    sub = LANES if part % LANES == 0 else part
    pieces = part // sub
    if pieces % 5 or pieces < 25:
        return sub, pieces, 1, [pieces], pieces, [pieces - 1 + n_row], 0, 1, 0
    groups = []
    while sum(groups) + 12 < pieces:
        groups.append(6)
    left = pieces - sum(groups)
    groups += [left - left // 2 + left % 2, left // 2 - left % 2] if left > 6 else [left]
    lead = sum(groups[:2])
    lag, stride = 3, 5
    total = pieces + lag + stride * (n_row - 1) - lead
    parts = [6, 6]
    total -= 12
    for g in range(2, len(groups)):
        parts.append(total // (len(groups) - g))
        total -= parts[-1]
    return sub, pieces, 5, groups, lead, parts, lag, stride, pieces - 3


def move_kernel(n_row, n_col, shape, corner, edge, sketch, sums, gram, cols, ring, images, mine, away, near, upper, lower, rows, scratch, square, land, piece, *sems):
    (load_sem, near_send, near_recv, chain_send, upper_recv, lower_recv,
     cast_send, cast_recv, back_send, back_recv, swap_send, swap_recv,
     fold_send, fold_recv, part_send, part_recv, full_send, full_recv) = sems
    sub, pieces, tiles, groups, lead, parts, lag, stride, hold = shape
    ratio = n_col // n_row
    me_row, me_col = lax.axis_index("row"), lax.axis_index("col")
    place, half = me_col // ratio, lax.rem(me_col, ratio)
    part = cols.shape[1]
    chunk = part // tiles
    tmp = scratch if pieces > 1 else images.at[0, 0, 0]
    per_tile = pieces // tiles

    owner = place == me_row
    has_upper = jnp.logical_and(place >= me_row, place < n_row - 1)
    has_lower = jnp.logical_and(place <= me_row, place > 0)
    to_lower, to_upper = place > me_row, place < me_row
    back_up = jnp.logical_and(place >= me_row, place < n_row - 1)
    back_down = jnp.logical_and(place <= me_row, place > 0)

    def partner(d):
        return (me_row, place * ratio + lax.rem(half + d, ratio))

    def peer(d):
        return (lax.rem(me_row + d, n_row), me_col)

    def column(d):
        return (me_row, lax.rem(me_col + d, n_col))

    up_id = (me_row, lax.rem(me_col + ratio, n_col))
    down_id = (me_row, lax.rem(me_col + n_col - ratio, n_col))

    def remote(source, target, send, recv, device):
        return pltpu.make_async_remote_copy(
            src_ref=source, dst_ref=target, send_sem=send, recv_sem=recv,
            device_id=device, device_id_type=pl.DeviceIdType.MESH,
        )

    def span(s, count=1):
        if pieces == 1:
            return pl.ds(0, sub)
        return pl.ds(pl.multiple_of(s * sub, sub), count * sub)

    def near_copy(d, s):
        return remote(away.at[d - 1, :, span(s)], near.at[d - 1, :, span(s)],
                      near_send.at[d - 1, s], near_recv.at[d - 1, s], partner(d))

    def down_copy(s):
        return remote(mine.at[:, span(s)], upper.at[:, span(s)], chain_send.at[s], upper_recv.at[s], down_id)

    def up_copy(s):
        return remote(mine.at[:, span(s)], lower.at[:, span(s)], chain_send.at[s], lower_recv.at[s], up_id)

    def cast_copy(d, s):
        return remote(rows.at[0, :, span(s)], cols.at[:, span(s)], cast_send.at[d - 1, s], cast_recv.at[s], peer(d))

    def back_copy(way, s):
        return remote(rows.at[0, :, span(s)], rows.at[0, :, span(s)], back_send.at[way, s], back_recv.at[s],
                      up_id if way else down_id)

    def swap_copy(d, s):
        return remote(rows.at[0, :, span(s)], rows.at[ratio - d, :, span(s)],
                      swap_send.at[d - 1, s], swap_recv.at[ratio - d - 1, s], partner(d))

    starts = [sum(groups[:g]) for g in range(len(groups))]

    def load(matrix, t, g, slot):
        k0, width = starts[g] * sub, groups[g] * sub
        copies = []
        for pos in range(ratio):
            at = pl.multiple_of(lax.rem(half + pos, ratio) * part + t * chunk, TILE * 2)
            copies.append(pltpu.make_async_copy(
                matrix.at[pl.ds(at, chunk), k0 : k0 + width], ring.at[slot, pos, :, 0:width], load_sem.at[slot, pos]))
        return copies

    def product(left, t, g, slot):
        k0, width = starts[g] * sub, groups[g] * sub
        operand = left[:, k0 : k0 + width]
        if chunk % LANES == 0:
            block = ring[slot, :, :, 0:width].reshape(ratio * chunk, width)
            found = across(operand, block)
            return [found[:, p * chunk : (p + 1) * chunk] for p in range(ratio)]
        return [across(operand, ring[slot, p, :, 0:width]) for p in range(ratio)]

    barrier = pltpu.get_barrier_semaphore()

    def greet(device):
        pl.semaphore_signal(barrier, inc=1, device_id=device, device_id_type=pl.DeviceIdType.MESH)

    n_groups = len(groups)
    steps = [("sample", g) for g in range(n_groups)]

    def start_sample(t, g, slot):
        for copy in load(corner, t, g, slot):
            copy.start()

    def start_image(m, t, g, slot):
        for copy in load(edge if m else corner, t, g, slot):
            copy.start()

    total_sample = tiles * n_groups

    def start_at(index):
        if index < total_sample:
            start_sample(index // n_groups, index % n_groups, index % SLOTS)
        else:
            index -= total_sample
            g, rest = divmod(index, 2 * tiles)
            start_image(rest % 2, rest // 2, g, (index + total_sample) % SLOTS)

    for index in range(AHEAD):
        start_at(index)
    for d in range(1, n_row):
        greet(peer(d))
    for d in range(1, n_col):
        greet(column(d))
    pl.semaphore_wait(barrier, n_row + n_col - 2)

    def gather(s):
        total = mine[:, span(s)].astype(jnp.float32)
        for d in range(1, ratio):
            near_copy(d, s).wait_recv()
            total += near[d - 1, :, span(s)].astype(jnp.float32)
        tmp[...] = total

        @pl.when(has_upper)
        def _():
            down_copy(s).wait_recv()
            tmp[...] += upper[:, span(s)].astype(jnp.float32)

        @pl.when(has_lower)
        def _():
            up_copy(s).wait_recv()
            tmp[...] += lower[:, span(s)].astype(jnp.float32)

        @pl.when(owner)
        def _():
            value = tmp[...].astype(jnp.bfloat16)
            rows[0, :, span(s)] = value
            cols[:, span(s)] = value
            for d in range(1, n_row):
                cast_copy(d, s).start()

            @pl.when(place < n_row - 1)
            def _():
                back_copy(1, s).start()

            @pl.when(place > 0)
            def _():
                back_copy(0, s).start()

        @pl.when(to_lower)
        def _():
            mine[:, span(s)] = tmp[...].astype(jnp.bfloat16)
            down_copy(s).start()

        @pl.when(to_upper)
        def _():
            mine[:, span(s)] = tmp[...].astype(jnp.bfloat16)
            up_copy(s).start()

    prompt = pieces - 10 if pieces > 10 else pieces

    def hand_back(s):
        @pl.when(jnp.logical_not(owner))
        def _():
            back_copy(0, s).wait_recv()

            @pl.when(jnp.logical_and(to_lower, place < n_row - 1))
            def _():
                back_copy(1, s).start()

            @pl.when(jnp.logical_and(to_upper, place > 0))
            def _():
                back_copy(0, s).start()

    def swap(first, last):
        for s in range(first, last):
            for d in range(1, ratio):
                swap_copy(d, s).start()

    wait = lag + stride * jnp.abs(place - me_row)

    def advance(first, p):
        if first < pieces:
            @pl.when(p < pieces)
            def _():
                gather(p)

        @pl.when(jnp.logical_and(p >= wait, p < wait + pieces))
        def _():
            hand_back(p - wait)

        turn = p - jnp.maximum(wait, hold)

        @pl.when(jnp.logical_and(turn >= 0, turn < prompt))
        def _():
            for d in range(1, ratio):
                swap_copy(d, turn).start()

    def positions(first, start, stop):
        def one(p, carry):
            advance(first, p)
            return carry

        lax.fori_loop(start, stop, one, 0)

    source = jnp.where(to_lower, n_row - 1 - place, jnp.where(to_upper, place, jnp.maximum(n_row - 1 - place, place)))

    def early(t):
        return jnp.clip(2 * t - 1 - 2 * source, 0, lead) if tiles > 1 else 0

    begin = jnp.maximum(groups[0], lead - 2 * source)
    floor = max(groups[0], lead - 2 * (n_row - 1))

    def sample_tile(t, carry):
        for g in range(n_groups):
            index = t * n_groups + g
            slot = lax.rem(index, SLOTS)
            for copy in load(corner, t, g, slot):
                copy.wait()
            later = g + AHEAD
            if later < n_groups:
                start_sample(t, later, lax.rem(index + AHEAD, SLOTS))
            else:
                later_t, later_g = t + later // n_groups, later % n_groups

                @pl.when(later_t < tiles)
                def _():
                    start_sample(later_t, later_g, lax.rem(index + AHEAD, SLOTS))

            found = product(sketch, t, g, slot)
            if g > 0:
                found = [images[0, 0, p] + found[p] for p in range(ratio)]
            if g < n_groups - 1:
                for p in range(ratio):
                    images[0, 0, p] = found[p]
            else:
                at = span(t * per_tile, per_tile)
                mine[:, at] = found[0].astype(jnp.bfloat16)
                for d in range(1, ratio):
                    away[d - 1, :, at] = found[d].astype(jnp.bfloat16)
        for d in range(1, ratio):
            for i in range(per_tile):
                near_copy(d, t * per_tile + i).start()
        if tiles > 1:
            positions(0, early(t - 1), early(t))
        return carry

    lax.fori_loop(0, tiles, sample_tile, 0)
    for index in range(AHEAD):
        start_at(total_sample + index)
    positions(0, early(tiles - 1), begin)

    first = 0
    for g in range(n_groups):
        for i in range(groups[g]):
            s = starts[g] + i

            @pl.when(jnp.logical_not(owner))
            def _():
                cast_copy(1, s).wait_recv()

        every = parts[g] // tiles

        def image_tile(t, carry):
            for m in range(2):
                index = total_sample + (g * tiles + t) * 2 + m
                slot = lax.rem(index, SLOTS)
                for copy in load(edge if m else corner, t, g, slot):
                    copy.wait()
                ahead = t * 2 + m + AHEAD
                into = lax.rem(index + AHEAD, SLOTS)

                @pl.when(ahead < 2 * tiles)
                def _():
                    start_image(m, t + 1, g, into)

                if g + 1 < n_groups:
                    @pl.when(ahead >= 2 * tiles)
                    def _():
                        start_image(m, 0, g + 1, into)

                found = product(cols, t, g, slot)
                for p in range(ratio):
                    if g == 0:
                        images[m, t, p] = found[p]
                    else:
                        images[m, t, p] += found[p]
            for i in range(every):
                advance(floor + first, begin + first + t * every + i)
            return carry

        lax.fori_loop(0, tiles, image_tile, 0)
        tail = parts[g] - every * tiles
        if tail:
            positions(floor + first, begin + first + every * tiles, begin + first + parts[g])
        first += parts[g]

    width, padded = cols.shape[0], square.shape[0]
    big = padded // n_row
    small = big // n_col

    def at_rows(index, size):
        return pl.ds(pl.multiple_of(index, TILE), size)

    square[0:width, :] = across(cols[...], cols[...])
    if padded > width:
        square[width:padded, :] = jnp.zeros((padded - width, width), jnp.float32)
    folds, pieces_out, fulls = [], [], []
    for d in range(1, n_col):
        chunk_at = me_row * big + lax.rem(me_col + d, n_col) * small
        folds.append(remote(square.at[at_rows(chunk_at, small), :], land.at[d - 1],
                            fold_send.at[d - 1], fold_recv.at[d - 1], column(d)))
        folds[-1].start()
    swap(prompt, min(prompt + 3, pieces))
    own = at_rows(me_row * big + me_col * small, small)
    summed = square[own, :]
    for d in range(1, n_col):
        folds[d - 1].wait_recv()
        summed += land[d - 1]
    piece[...] = summed
    for d in range(1, n_col):
        pieces_out.append(remote(piece, gram.at[own, :], part_send.at[d - 1], part_recv.at[d - 1], column(d)))
        pieces_out[-1].start()
    swap(min(prompt + 3, pieces), pieces)
    gram[own, :] = summed
    for d in range(1, n_col):
        pieces_out[d - 1].wait_recv()
    block = gram.at[at_rows(me_row * big, big), :]
    for d in range(1, n_row):
        fulls.append(remote(block, block, full_send.at[d - 1], full_recv.at[d - 1], peer(d)))
        fulls[-1].start()

    sums[...] = jnp.zeros_like(sums)

    def left_tile(t, carry):
        for d in range(1, ratio):
            for i in range(per_tile):
                swap_copy(d, t * per_tile + i).wait_recv()
        at = span(t * per_tile, per_tile)

        def both(p):
            return jnp.concatenate([images[m, t, p] for m in range(2)], axis=0).astype(jnp.bfloat16)

        if chunk % LANES == 0:
            left = jnp.concatenate([rows[p, :, at] for p in range(ratio)], axis=1)
            right = jnp.concatenate([both(p) for p in range(ratio)], axis=1)
            sums[...] += across(left, right)
        else:
            for p in range(ratio):
                sums[...] += across(rows[p, :, at], both(p))
        return carry

    lax.fori_loop(0, tiles, left_tile, 0)
    for sent in fulls:
        sent.wait_recv()
    for sent in folds + pieces_out + fulls:
        sent.wait_send()

    def finish(s, carry):
        for d in range(1, ratio):
            near_copy(d, s).wait_send()
            swap_copy(d, s).wait_send()

        @pl.when(owner)
        def _():
            for d in range(1, n_row):
                cast_copy(d, s).wait_send()

        @pl.when(jnp.logical_not(owner))
        def _():
            down_copy(s).wait_send()

        @pl.when(back_up)
        def _():
            back_copy(1, s).wait_send()

        @pl.when(back_down)
        def _():
            back_copy(0, s).wait_send()

        return carry

    lax.fori_loop(0, pieces, finish, 0)


def move(corner, edge, sketch):
    n_row, n_col = lax.axis_size("row"), lax.axis_size("col")
    height, part = corner.shape
    width = sketch.shape[0]
    ratio = n_col // n_row
    assert ratio * n_row == n_col and height == ratio * part
    shape = plan(part, n_row)
    sub, pieces, tiles, groups = shape[:4]
    chunk = part // tiles
    dma = pltpu.SemaphoreType.DMA
    half = jnp.bfloat16
    grain = n_row * n_col * TILE
    padded = -(-width // grain) * grain
    small = padded // (n_row * n_col)
    vmem = pl.BlockSpec(memory_space=pltpu.VMEM)
    hbm = pl.BlockSpec(memory_space=pl.ANY)
    return pl.pallas_call(
        functools.partial(move_kernel, n_row, n_col, shape),
        out_shape=(jax.ShapeDtypeStruct((width, 2 * width), jnp.float32),
                   jax.ShapeDtypeStruct((padded, width), jnp.float32)),
        in_specs=[hbm, hbm, vmem],
        out_specs=(vmem, vmem),
        scratch_shapes=[
            pltpu.VMEM((width, part), half),
            pltpu.VMEM((SLOTS, ratio, chunk, max(groups) * sub), half),
            pltpu.VMEM((2, tiles, ratio, width, chunk), jnp.float32),
            pltpu.VMEM((width, part), half),
            pltpu.VMEM((ratio - 1, width, part), half),
            pltpu.VMEM((ratio - 1, width, part), half),
            pltpu.VMEM((width, part), half),
            pltpu.VMEM((width, part), half),
            pltpu.VMEM((ratio, width, part), half),
            pltpu.VMEM((width, sub) if pieces > 1 else (TILE, LANES), jnp.float32),
            pltpu.VMEM((padded, width), jnp.float32),
            pltpu.VMEM((n_col - 1, small, width), jnp.float32),
            pltpu.VMEM((small, width), jnp.float32),
            dma((SLOTS, ratio)),
            dma((ratio - 1, pieces)), dma((ratio - 1, pieces)),
            dma((pieces,)), dma((pieces,)), dma((pieces,)),
            dma((n_row - 1, pieces)), dma((pieces,)),
            dma((2, pieces)), dma((pieces,)),
            dma((ratio - 1, pieces)), dma((ratio - 1, pieces)),
            dma((n_col - 1,)), dma((n_col - 1,)), dma((n_col - 1,)), dma((n_col - 1,)),
            dma((n_row - 1,)), dma((n_row - 1,)),
        ],
        compiler_params=pltpu.CompilerParams(
            collective_id=2, has_side_effects=True, vmem_limit_bytes=VMEM_LIMIT),
    )(corner, edge, sketch)


def eliminate(block):
    size = block.shape[0]
    count = size // TILE
    lane = lax.broadcasted_iota(jnp.int32, (TILE, BLOCK), 1)
    line = lax.broadcasted_iota(jnp.int32, (2 * TILE, BLOCK), 0)
    work = [block[t * TILE : (t + 1) * TILE, :] for t in range(count)]
    top = lax.broadcasted_iota(jnp.int32, (TILE, BLOCK), 0)
    other = [(lane == top + t * TILE).astype(jnp.float32) for t in range(count)]
    done = []
    for h in range(count):
        at = h * TILE
        tiles = [h, h + 1] if h + 1 < count else [h]
        high = len(tiles) * TILE
        pair = jnp.concatenate([work[t] for t in tiles], axis=0)
        held = jnp.concatenate([other[t] for t in tiles], axis=0)
        fixed = [jnp.broadcast_to(pair[:, at + k : at + k + 1], (high, BLOCK)) for k in range(TILE)]
        ids = line[:high]
        for k in range(TILE):
            scale = 1.0 / fixed[k][k : k + 1, :]
            factor = jnp.where(ids > k, fixed[k] * scale, 0.0)
            pair = pair - factor * pair[k : k + 1, :]
            held = held - factor * held[k : k + 1, :]
            for j in range(k + 1, TILE):
                fixed[j] = fixed[j] - factor * fixed[j][k : k + 1, :]
        pivot = fixed[0][:TILE]
        for k in range(1, TILE):
            pivot = jnp.where(top == k, fixed[k][:TILE], pivot)
        upper, extra = pair[:TILE], held[:TILE]
        done.append(extra / jnp.sqrt(pivot))
        if h + 1 < count:
            work[h + 1], other[h + 1] = pair[TILE:], held[TILE:]
        if h + 2 < count:
            low = (h + 2) * TILE
            both = jnp.concatenate([upper / pivot, extra / pivot], axis=1)
            update = lax.dot_general(
                jnp.where(lane >= low, upper, 0.0), both, (((0,), (0,)), ((), ())),
                precision=HIGHEST, preferred_element_type=jnp.float32)
            for t in range(h + 2, count):
                work[t] = work[t] - update[t * TILE : (t + 1) * TILE, :BLOCK]
                other[t] = other[t] - update[t * TILE : (t + 1) * TILE, BLOCK:]
    return jnp.concatenate(done, axis=0)


def finish_kernel(n_row, n_col, sums, gram, total, inverse_out, x, out, held, *rest):
    lands, sems = rest[:3], rest[3:]
    me_row, me_col = lax.axis_index("row"), lax.axis_index("col")
    inner, outer = lax.rem(me_row, 2), me_row // 2
    counts = [2, n_row // 2, n_col]
    mine = [inner, outer, me_col]

    def device(level, d):
        other = lax.rem(mine[level] + d, counts[level])
        return [(outer * 2 + other, me_col), (other * 2 + inner, me_col), (me_row, other)][level]

    def copy(source, target, send, recv, where):
        return pltpu.make_async_remote_copy(
            src_ref=source, dst_ref=target, send_sem=send, recv_sem=recv,
            device_id=where, device_id_type=pl.DeviceIdType.MESH,
        )

    barrier = pltpu.get_barrier_semaphore()
    for level in range(3):
        for d in range(1, counts[level]):
            pl.semaphore_signal(barrier, inc=1, device_id=device(level, d), device_id_type=pl.DeviceIdType.MESH)

    size = gram.shape[1]
    tall, wide = size // TILE, 2 * size // LANES
    for j in range(wide):
        x[j * tall : (j + 1) * tall] = sums[:, j * LANES : (j + 1) * LANES].reshape(tall, TILE, LANES)
    if x.shape[0] > tall * wide:
        x[tall * wide :] = jnp.zeros((x.shape[0] - tall * wide, TILE, LANES), jnp.float32)
    padded = held.shape[0]
    ids_r = lax.broadcasted_iota(jnp.int32, (padded, padded), 0)
    ids_c = lax.broadcasted_iota(jnp.int32, (padded, padded), 1)
    unit = (ids_r == ids_c).astype(jnp.float32)
    held[:, :padded] = unit
    held[:, padded:] = unit
    held[:size, :size] = gram[:size, :]

    bases, sizes = [0], []
    for level in range(3):
        sizes.append((sizes[-1] if sizes else x.shape[0]) // counts[level])
        bases.append(bases[-1] + mine[level] * sizes[-1])

    def scatter(level):
        m = sizes[level]
        return [copy(x.at[pl.ds(bases[level] + lax.rem(mine[level] + d, counts[level]) * m, m)],
                     lands[level].at[d - 1], sems[4 * level].at[d - 1], sems[4 * level + 1].at[d - 1], device(level, d))
                for d in range(1, counts[level])]

    def spread(level):
        block = out.at[pl.ds(bases[level + 1], sizes[level])]
        return [copy(block, block, sems[4 * level + 2].at[d - 1], sems[4 * level + 3].at[d - 1], device(level, d))
                for d in range(1, counts[level])]

    def fold(level):
        own = pl.ds(bases[level + 1], sizes[level])
        value = x[own]
        for d, sent in enumerate(scatter(level)):
            sent.wait_recv()
            value += lands[level][d]
        if level == 2:
            out[own] = value
        else:
            x[own] = value

    def begin(copies):
        for sent in copies:
            sent.start()

    def arrive(copies):
        for sent in copies:
            sent.wait_recv()

    pl.semaphore_wait(barrier, sum(counts) - 3)
    begin(scatter(0))
    fold(0)
    begin(scatter(1))

    def stage(i):
        if i == 0:
            fold(1)
            begin(scatter(2))
        elif i == 1:
            fold(2)
            begin(spread(2))
        elif i == 2:
            arrive(spread(2))
            begin(spread(1))
        else:
            arrive(spread(1))
            begin(spread(0))

    blocks = padded // BLOCK

    def one(k, carry):
        at = pl.multiple_of(k * BLOCK, BLOCK)
        inverse = eliminate(held[pl.ds(at, BLOCK), pl.ds(at, BLOCK)])
        strip = jnp.dot(inverse, held[pl.ds(at, BLOCK), :], precision=HIGHEST, preferred_element_type=jnp.float32)
        held[pl.ds(at, BLOCK), :] = strip

        def trail(i, inner_carry):
            low = pl.multiple_of(i * BLOCK, BLOCK)
            side = held[pl.ds(at, BLOCK), pl.ds(low, BLOCK)]
            held[pl.ds(low, BLOCK), :] -= jnp.dot(
                side.T, held[pl.ds(at, BLOCK), :], precision=HIGHEST, preferred_element_type=jnp.float32
            )
            return inner_carry

        lax.fori_loop(k + 1, blocks, trail, 0)
        for i in range(4):
            @pl.when(k == min(i, blocks - 1))
            def _():
                stage(i)

        return carry

    lax.fori_loop(0, blocks, one, 0)
    inverse_out[...] = held[:size, padded : padded + size]
    arrive(spread(0))
    for j in range(wide):
        total[:, j * LANES : (j + 1) * LANES] = out[j * tall : (j + 1) * tall].reshape(size, LANES)
    for level in range(3):
        for sent in scatter(level) + spread(level):
            sent.wait_send()


def finish(sums, gram):
    n_row, n_col = lax.axis_size("row"), lax.axis_size("col")
    width = gram.shape[1]
    assert n_row % 2 == 0 and width % TILE == 0 and 2 * width % LANES == 0
    padded = -(-width // BLOCK) * BLOCK
    tiles = width * 2 * width // (TILE * LANES)
    tiles = -(-tiles // (n_row * n_col)) * n_row * n_col
    counts = [2, n_row // 2, n_col]
    dma = pltpu.SemaphoreType.DMA
    lands, sems, size = [], [], tiles
    for count in counts:
        size //= count
        lands.append(pltpu.VMEM((count - 1, size, TILE, LANES), jnp.float32))
        sems += [dma((count - 1,))] * 4
    vmem = pl.BlockSpec(memory_space=pltpu.VMEM)
    return pl.pallas_call(
        functools.partial(finish_kernel, n_row, n_col),
        out_shape=(jax.ShapeDtypeStruct((width, 2 * width), jnp.float32),
                   jax.ShapeDtypeStruct((width, width), jnp.float32)),
        in_specs=[vmem, vmem],
        out_specs=(vmem, vmem),
        scratch_shapes=[
            pltpu.VMEM((tiles, TILE, LANES), jnp.float32),
            pltpu.VMEM((tiles, TILE, LANES), jnp.float32),
            pltpu.VMEM((padded, 2 * padded), jnp.float32),
        ] + lands + sems,
        compiler_params=pltpu.CompilerParams(collective_id=1, has_side_effects=True),
    )(sums, gram)


def body(corner, edge, sketch):
    sums, gram = move(corner, edge, sketch.T)
    total, inverse = finish(sums, gram)
    width = gram.shape[1]
    inverse = inverse[width - RANK :]
    half = jnp.dot(inverse, total, precision=HIGHEST)

    def turn(side):
        return lax.dot_general(side, inverse, (((1,), (1,)), ((), ())), precision=HIGHEST)

    return turn(half[:, :width]), turn(half[:, width:])


def solution(mesh):
    placed = (P("row", "col"), P("row", "col"), P("col", None))
    return jax.shard_map(body, mesh=mesh, in_specs=placed, out_specs=(P(), P()), check_vma=False)
```

```python
import functools

import jax
import jax.numpy as jnp
from jax import lax
from jax.experimental import pallas as pl
from jax.experimental.pallas import tpu as pltpu
from jax.sharding import PartitionSpec as P

RANK = 400
HIGHEST = lax.Precision.HIGHEST
BLOCK = 128
TILE = 8
LANES = 128
SLOTS = 3
AHEAD = 2
VMEM_LIMIT = 67043328
PROMPT = 12
LATE = 6


def across(left, right):
    return lax.dot_general(left, right, (((1,), (1,)), ((), ())), preferred_element_type=jnp.float32)


def plan(part, n_row):
    sub = LANES if part % LANES == 0 else part
    pieces = part // sub
    if pieces % 5 or pieces < 25:
        return sub, pieces, 1, [pieces], pieces, [pieces - 1 + n_row], 0, 1, 0
    groups = []
    while sum(groups) + 12 < pieces:
        groups.append(6)
    left = pieces - sum(groups)
    groups += [left - left // 2 + left % 2, left // 2 - left % 2] if left > 6 else [left]
    lead = sum(groups[:2])
    lag, stride = 3, 5
    total = pieces + lag + stride * (n_row - 1) - lead
    parts = [6, 6]
    total -= 12
    for g in range(2, len(groups)):
        parts.append(total // (len(groups) - g))
        total -= parts[-1]
    return sub, pieces, 5, groups, lead, parts, lag, stride, pieces - 3


def move_kernel(n_row, n_col, shape, corner, edge, sketch, sums, gram, cols, ring, images, mine, away, near, upper, lower, rows, scratch, square, land, piece, *sems):
    (load_sem, near_send, near_recv, chain_send, upper_recv, lower_recv,
     cast_send, cast_recv, back_send, back_recv, swap_send, swap_recv,
     fold_send, fold_recv, part_send, part_recv, full_send, full_recv) = sems
    sub, pieces, tiles, groups, lead, parts, lag, stride, hold = shape
    ratio = n_col // n_row
    me_row, me_col = lax.axis_index("row"), lax.axis_index("col")
    place, half = me_col // ratio, lax.rem(me_col, ratio)
    part = cols.shape[1]
    chunk = part // tiles
    tmp = scratch if pieces > 1 else images.at[0, 0, 0]
    per_tile = pieces // tiles

    owner = place == me_row
    has_upper = jnp.logical_and(place >= me_row, place < n_row - 1)
    has_lower = jnp.logical_and(place <= me_row, place > 0)
    to_lower, to_upper = place > me_row, place < me_row
    back_up = jnp.logical_and(place >= me_row, place < n_row - 1)
    back_down = jnp.logical_and(place <= me_row, place > 0)

    def partner(d):
        return (me_row, place * ratio + lax.rem(half + d, ratio))

    def peer(d):
        return (lax.rem(me_row + d, n_row), me_col)

    def column(d):
        return (me_row, lax.rem(me_col + d, n_col))

    up_id = (me_row, lax.rem(me_col + ratio, n_col))
    down_id = (me_row, lax.rem(me_col + n_col - ratio, n_col))

    def remote(source, target, send, recv, device):
        return pltpu.make_async_remote_copy(
            src_ref=source, dst_ref=target, send_sem=send, recv_sem=recv,
            device_id=device, device_id_type=pl.DeviceIdType.MESH,
        )

    def span(s, count=1):
        if pieces == 1:
            return pl.ds(0, sub)
        return pl.ds(pl.multiple_of(s * sub, sub), count * sub)

    def near_copy(d, s):
        return remote(away.at[d - 1, :, span(s)], near.at[d - 1, :, span(s)],
                      near_send.at[d - 1, s], near_recv.at[d - 1, s], partner(d))

    def down_copy(s):
        return remote(mine.at[:, span(s)], upper.at[:, span(s)], chain_send.at[s], upper_recv.at[s], down_id)

    def up_copy(s):
        return remote(mine.at[:, span(s)], lower.at[:, span(s)], chain_send.at[s], lower_recv.at[s], up_id)

    def cast_copy(d, s):
        return remote(rows.at[0, :, span(s)], cols.at[:, span(s)], cast_send.at[d - 1, s], cast_recv.at[s], peer(d))

    def back_copy(way, s):
        return remote(rows.at[0, :, span(s)], rows.at[0, :, span(s)], back_send.at[way, s], back_recv.at[s],
                      up_id if way else down_id)

    def swap_copy(d, s):
        return remote(rows.at[0, :, span(s)], rows.at[ratio - d, :, span(s)],
                      swap_send.at[d - 1, s], swap_recv.at[ratio - d - 1, s], partner(d))

    starts = [sum(groups[:g]) for g in range(len(groups))]

    def load(matrix, t, g, slot):
        k0, width = starts[g] * sub, groups[g] * sub
        copies = []
        for pos in range(ratio):
            at = pl.multiple_of(lax.rem(half + pos, ratio) * part + t * chunk, TILE * 2)
            copies.append(pltpu.make_async_copy(
                matrix.at[pl.ds(at, chunk), k0 : k0 + width], ring.at[slot, pos, :, 0:width], load_sem.at[slot, pos]))
        return copies

    def product(left, t, g, slot):
        k0, width = starts[g] * sub, groups[g] * sub
        operand = left[:, k0 : k0 + width]
        if chunk % LANES == 0:
            block = ring[slot, :, :, 0:width].reshape(ratio * chunk, width)
            found = across(operand, block)
            return [found[:, p * chunk : (p + 1) * chunk] for p in range(ratio)]
        return [across(operand, ring[slot, p, :, 0:width]) for p in range(ratio)]

    barrier = pltpu.get_barrier_semaphore()

    def greet(device):
        pl.semaphore_signal(barrier, inc=1, device_id=device, device_id_type=pl.DeviceIdType.MESH)

    n_groups = len(groups)
    steps = [("sample", g) for g in range(n_groups)]

    def start_sample(t, g, slot):
        for copy in load(corner, t, g, slot):
            copy.start()

    def start_image(m, t, g, slot):
        for copy in load(edge if m else corner, t, g, slot):
            copy.start()

    total_sample = tiles * n_groups

    def start_at(index):
        if index < total_sample:
            start_sample(index // n_groups, index % n_groups, index % SLOTS)
        else:
            index -= total_sample
            g, rest = divmod(index, 2 * tiles)
            start_image(rest % 2, rest // 2, g, (index + total_sample) % SLOTS)

    for index in range(AHEAD):
        start_at(index)
    for d in range(1, n_row):
        greet(peer(d))
    for d in range(1, n_col):
        greet(column(d))

    def gather(s):
        total = mine[:, span(s)].astype(jnp.float32)
        for d in range(1, ratio):
            near_copy(d, s).wait_recv()
            total += near[d - 1, :, span(s)].astype(jnp.float32)
        tmp[...] = total

        @pl.when(has_upper)
        def _():
            down_copy(s).wait_recv()
            tmp[...] += upper[:, span(s)].astype(jnp.float32)

        @pl.when(has_lower)
        def _():
            up_copy(s).wait_recv()
            tmp[...] += lower[:, span(s)].astype(jnp.float32)

        @pl.when(owner)
        def _():
            value = tmp[...].astype(jnp.bfloat16)
            rows[0, :, span(s)] = value
            cols[:, span(s)] = value
            for d in range(1, n_row):
                cast_copy(d, s).start()

            @pl.when(place < n_row - 1)
            def _():
                back_copy(1, s).start()

            @pl.when(place > 0)
            def _():
                back_copy(0, s).start()

        @pl.when(to_lower)
        def _():
            mine[:, span(s)] = tmp[...].astype(jnp.bfloat16)
            down_copy(s).start()

        @pl.when(to_upper)
        def _():
            mine[:, span(s)] = tmp[...].astype(jnp.bfloat16)
            up_copy(s).start()

    prompt = PROMPT if pieces > PROMPT else pieces
    late = min(prompt + LATE, pieces)

    def hand_back(s):
        @pl.when(jnp.logical_not(owner))
        def _():
            back_copy(0, s).wait_recv()

            @pl.when(jnp.logical_and(to_lower, place < n_row - 1))
            def _():
                back_copy(1, s).start()

            @pl.when(jnp.logical_and(to_upper, place > 0))
            def _():
                back_copy(0, s).start()

    def swap(first, last):
        for s in range(first, last):
            for d in range(1, ratio):
                swap_copy(d, s).start()

    wait = lag + stride * jnp.abs(place - me_row)

    def advance(first, p):
        if first < pieces:
            @pl.when(p < pieces)
            def _():
                gather(p)

        @pl.when(jnp.logical_and(p >= wait, p < wait + pieces))
        def _():
            hand_back(p - wait)

        turn = p - jnp.maximum(wait, hold)

        @pl.when(jnp.logical_and(turn >= 0, turn < prompt))
        def _():
            for d in range(1, ratio):
                swap_copy(d, turn).start()

    def positions(first, start, stop):
        def one(p, carry):
            advance(first, p)
            return carry

        lax.fori_loop(start, stop, one, 0)

    source = jnp.where(to_lower, n_row - 1 - place, jnp.where(to_upper, place, jnp.maximum(n_row - 1 - place, place)))

    def early(t):
        return jnp.clip(2 * t - 1 - 2 * source, 0, lead) if tiles > 1 else 0

    begin = jnp.maximum(groups[0], lead - 2 * source)
    floor = max(groups[0], lead - 2 * (n_row - 1))

    def sample_tile(t, carry):
        for g in range(n_groups):
            index = t * n_groups + g
            slot = lax.rem(index, SLOTS)
            for copy in load(corner, t, g, slot):
                copy.wait()
            later = g + AHEAD
            if later < n_groups:
                start_sample(t, later, lax.rem(index + AHEAD, SLOTS))
            else:
                later_t, later_g = t + later // n_groups, later % n_groups

                @pl.when(later_t < tiles)
                def _():
                    start_sample(later_t, later_g, lax.rem(index + AHEAD, SLOTS))

            found = product(sketch, t, g, slot)
            if g > 0:
                found = [images[0, 0, p] + found[p] for p in range(ratio)]
            if g < n_groups - 1:
                for p in range(ratio):
                    images[0, 0, p] = found[p]
            else:
                at = span(t * per_tile, per_tile)
                mine[:, at] = found[0].astype(jnp.bfloat16)
                for d in range(1, ratio):
                    away[d - 1, :, at] = found[d].astype(jnp.bfloat16)

        @pl.when(t == 0)
        def _():
            pl.semaphore_wait(barrier, n_row + n_col - 2)

        for d in range(1, ratio):
            for i in range(per_tile):
                near_copy(d, t * per_tile + i).start()
        if tiles > 1:
            positions(0, early(t - 1), early(t))
        return carry

    lax.fori_loop(0, tiles, sample_tile, 0)
    for index in range(AHEAD):
        start_at(total_sample + index)
    positions(0, early(tiles - 1), begin)

    width, padded = cols.shape[0], square.shape[0]
    big = padded // n_row
    small = big // n_col

    def at_rows(index, size):
        return pl.ds(pl.multiple_of(index, TILE), size)

    folds, pieces_out, fulls = [], [], []

    def start_gram():
        square[0:width, :] = across(cols[...], cols[...])
        if padded > width:
            square[width:padded, :] = jnp.zeros((padded - width, width), jnp.float32)
        for d in range(1, n_col):
            chunk_at = me_row * big + lax.rem(me_col + d, n_col) * small
            folds.append(remote(square.at[at_rows(chunk_at, small), :], land.at[d - 1],
                                fold_send.at[d - 1], fold_recv.at[d - 1], column(d)))
            folds[-1].start()
        swap(prompt, late)

    first = 0
    for g in range(n_groups):
        for i in range(groups[g]):
            s = starts[g] + i

            @pl.when(jnp.logical_not(owner))
            def _():
                cast_copy(1, s).wait_recv()

        if g == n_groups - 1:
            start_gram()
        every = parts[g] // tiles

        def image_tile(t, carry):
            for m in range(2):
                index = total_sample + (g * tiles + t) * 2 + m
                slot = lax.rem(index, SLOTS)
                for copy in load(edge if m else corner, t, g, slot):
                    copy.wait()
                ahead = t * 2 + m + AHEAD
                into = lax.rem(index + AHEAD, SLOTS)

                @pl.when(ahead < 2 * tiles)
                def _():
                    start_image(m, t + 1, g, into)

                if g + 1 < n_groups:
                    @pl.when(ahead >= 2 * tiles)
                    def _():
                        start_image(m, 0, g + 1, into)

                found = product(cols, t, g, slot)
                for p in range(ratio):
                    if g == 0:
                        images[m, t, p] = found[p]
                    else:
                        images[m, t, p] += found[p]
            for i in range(every):
                advance(floor + first, begin + first + t * every + i)
            return carry

        lax.fori_loop(0, tiles, image_tile, 0)
        tail = parts[g] - every * tiles
        if tail:
            positions(floor + first, begin + first + every * tiles, begin + first + parts[g])
        first += parts[g]

    sums[...] = jnp.zeros_like(sums)

    def left(p, t):
        images_t = jnp.concatenate([images[m, t, p] for m in range(2)], axis=0).astype(jnp.bfloat16)
        sums[...] += across(rows[p, :, span(t * per_tile, per_tile)], images_t)

    def own_tile(t, carry):
        left(0, t)
        return carry

    def other_tile(t, carry):
        for d in range(1, ratio):
            for i in range(per_tile):
                swap_copy(d, t * per_tile + i).wait_recv()
        for p in range(1, ratio):
            left(p, t)
        return carry

    lax.fori_loop(0, tiles, own_tile, 0)
    own = at_rows(me_row * big + me_col * small, small)
    summed = square[own, :]
    for d in range(1, n_col):
        folds[d - 1].wait_recv()
        summed += land[d - 1]
    piece[...] = summed
    for d in range(1, n_col):
        pieces_out.append(remote(piece, gram.at[own, :], part_send.at[d - 1], part_recv.at[d - 1], column(d)))
        pieces_out[-1].start()
    swap(late, pieces)
    gram[own, :] = summed
    first_tiles = min(3, tiles)
    lax.fori_loop(0, first_tiles, other_tile, 0)
    for d in range(1, n_col):
        pieces_out[d - 1].wait_recv()
    block = gram.at[at_rows(me_row * big, big), :]
    for d in range(1, n_row):
        fulls.append(remote(block, block, full_send.at[d - 1], full_recv.at[d - 1], peer(d)))
        fulls[-1].start()
    if first_tiles < tiles:
        lax.fori_loop(first_tiles, tiles, other_tile, 0)
    for sent in fulls:
        sent.wait_recv()
    for sent in folds + pieces_out + fulls:
        sent.wait_send()

    def finish(s, carry):
        for d in range(1, ratio):
            near_copy(d, s).wait_send()
            swap_copy(d, s).wait_send()

        @pl.when(owner)
        def _():
            for d in range(1, n_row):
                cast_copy(d, s).wait_send()

        @pl.when(jnp.logical_not(owner))
        def _():
            down_copy(s).wait_send()

        @pl.when(back_up)
        def _():
            back_copy(1, s).wait_send()

        @pl.when(back_down)
        def _():
            back_copy(0, s).wait_send()

        return carry

    lax.fori_loop(0, pieces, finish, 0)


def move(corner, edge, sketch):
    n_row, n_col = lax.axis_size("row"), lax.axis_size("col")
    height, part = corner.shape
    width = sketch.shape[0]
    ratio = n_col // n_row
    assert ratio * n_row == n_col and height == ratio * part
    shape = plan(part, n_row)
    sub, pieces, tiles, groups = shape[:4]
    chunk = part // tiles
    dma = pltpu.SemaphoreType.DMA
    half = jnp.bfloat16
    grain = n_row * n_col * TILE
    padded = -(-width // grain) * grain
    small = padded // (n_row * n_col)
    vmem = pl.BlockSpec(memory_space=pltpu.VMEM)
    hbm = pl.BlockSpec(memory_space=pl.ANY)
    return pl.pallas_call(
        functools.partial(move_kernel, n_row, n_col, shape),
        out_shape=(jax.ShapeDtypeStruct((width, 2 * width), jnp.float32),
                   jax.ShapeDtypeStruct((padded, width), jnp.float32)),
        in_specs=[hbm, hbm, vmem],
        out_specs=(vmem, vmem),
        scratch_shapes=[
            pltpu.VMEM((width, part), half),
            pltpu.VMEM((SLOTS, ratio, chunk, max(groups) * sub), half),
            pltpu.VMEM((2, tiles, ratio, width, chunk), jnp.float32),
            pltpu.VMEM((width, part), half),
            pltpu.VMEM((ratio - 1, width, part), half),
            pltpu.VMEM((ratio - 1, width, part), half),
            pltpu.VMEM((width, part), half),
            pltpu.VMEM((width, part), half),
            pltpu.VMEM((ratio, width, part), half),
            pltpu.VMEM((width, sub) if pieces > 1 else (TILE, LANES), jnp.float32),
            pltpu.VMEM((padded, width), jnp.float32),
            pltpu.VMEM((n_col - 1, small, width), jnp.float32),
            pltpu.VMEM((small, width), jnp.float32),
            dma((SLOTS, ratio)),
            dma((ratio - 1, pieces)), dma((ratio - 1, pieces)),
            dma((pieces,)), dma((pieces,)), dma((pieces,)),
            dma((n_row - 1, pieces)), dma((pieces,)),
            dma((2, pieces)), dma((pieces,)),
            dma((ratio - 1, pieces)), dma((ratio - 1, pieces)),
            dma((n_col - 1,)), dma((n_col - 1,)), dma((n_col - 1,)), dma((n_col - 1,)),
            dma((n_row - 1,)), dma((n_row - 1,)),
        ],
        compiler_params=pltpu.CompilerParams(
            collective_id=2, has_side_effects=True, vmem_limit_bytes=VMEM_LIMIT),
    )(corner, edge, sketch)


def eliminate(block):
    size = block.shape[0]
    count = size // TILE
    lane = lax.broadcasted_iota(jnp.int32, (TILE, BLOCK), 1)
    line = lax.broadcasted_iota(jnp.int32, (2 * TILE, BLOCK), 0)
    work = [block[t * TILE : (t + 1) * TILE, :] for t in range(count)]
    top = lax.broadcasted_iota(jnp.int32, (TILE, BLOCK), 0)
    other = [(lane == top + t * TILE).astype(jnp.float32) for t in range(count)]
    done = []
    for h in range(count):
        at = h * TILE
        tiles = [h, h + 1] if h + 1 < count else [h]
        high = len(tiles) * TILE
        pair = jnp.concatenate([work[t] for t in tiles], axis=0)
        held = jnp.concatenate([other[t] for t in tiles], axis=0)
        fixed = [jnp.broadcast_to(pair[:, at + k : at + k + 1], (high, BLOCK)) for k in range(TILE)]
        ids = line[:high]
        for k in range(TILE):
            scale = 1.0 / fixed[k][k : k + 1, :]
            factor = jnp.where(ids > k, fixed[k] * scale, 0.0)
            pair = pair - factor * pair[k : k + 1, :]
            held = held - factor * held[k : k + 1, :]
            for j in range(k + 1, TILE):
                fixed[j] = fixed[j] - factor * fixed[j][k : k + 1, :]
        pivot = fixed[0][:TILE]
        for k in range(1, TILE):
            pivot = jnp.where(top == k, fixed[k][:TILE], pivot)
        upper, extra = pair[:TILE], held[:TILE]
        done.append(extra / jnp.sqrt(pivot))
        if h + 1 < count:
            work[h + 1], other[h + 1] = pair[TILE:], held[TILE:]
        if h + 2 < count:
            low = (h + 2) * TILE
            both = jnp.concatenate([upper / pivot, extra / pivot], axis=1)
            update = lax.dot_general(
                jnp.where(lane >= low, upper, 0.0), both, (((0,), (0,)), ((), ())),
                precision=HIGHEST, preferred_element_type=jnp.float32)
            for t in range(h + 2, count):
                work[t] = work[t] - update[t * TILE : (t + 1) * TILE, :BLOCK]
                other[t] = other[t] - update[t * TILE : (t + 1) * TILE, BLOCK:]
    return jnp.concatenate(done, axis=0)


def finish_kernel(n_row, n_col, shares, sums, gram, total, inverse_out, x, out, held, *rest):
    orders = ((0, 1, 2), (0, 2, 1))
    lands, sems = rest[:6], rest[6:]
    me_row, me_col = lax.axis_index("row"), lax.axis_index("col")
    inner, outer = lax.rem(me_row, 2), me_row // 2
    counts = [2, n_row // 2, n_col]
    mine = [inner, outer, me_col]

    def device(level, d):
        other = lax.rem(mine[level] + d, counts[level])
        return [(outer * 2 + other, me_col), (other * 2 + inner, me_col), (me_row, other)][level]

    def copy(source, target, send, recv, where):
        return pltpu.make_async_remote_copy(
            src_ref=source, dst_ref=target, send_sem=send, recv_sem=recv,
            device_id=where, device_id_type=pl.DeviceIdType.MESH,
        )

    barrier = pltpu.get_barrier_semaphore()
    for level in range(3):
        for d in range(1, counts[level]):
            pl.semaphore_signal(barrier, inc=1, device_id=device(level, d), device_id_type=pl.DeviceIdType.MESH)

    size = gram.shape[1]
    tall, wide = size // TILE, 2 * size // LANES
    for j in range(wide):
        x[j * tall : (j + 1) * tall] = sums[:, j * LANES : (j + 1) * LANES].reshape(tall, TILE, LANES)
    if x.shape[0] > tall * wide:
        x[tall * wide :] = jnp.zeros((x.shape[0] - tall * wide, TILE, LANES), jnp.float32)
    padded = held.shape[0]
    ids_r = lax.broadcasted_iota(jnp.int32, (padded, padded), 0)
    ids_c = lax.broadcasted_iota(jnp.int32, (padded, padded), 1)
    unit = (ids_r == ids_c).astype(jnp.float32)
    held[:, :padded] = unit
    held[:, padded:] = unit
    held[:size, :size] = gram[:size, :]

    spots = []
    for group, order in enumerate(orders):
        base, size_now = shares[0] * group, shares[group]
        steps = []
        for level in order:
            size_now //= counts[level]
            steps.append((base, base + mine[level] * size_now, size_now))
            base = base + mine[level] * size_now
        spots.append(steps)

    def links(group, step):
        n = 3 * group + step
        return lands[n], sems[4 * n : 4 * n + 4]

    def scatter(step):
        copies = []
        for group, order in enumerate(orders):
            level, (base, _, m) = order[step], spots[group][step]
            land, (send, recv, _, _) = links(group, step)
            copies += [copy(x.at[pl.ds(base + lax.rem(mine[level] + d, counts[level]) * m, m)],
                            land.at[d - 1], send.at[d - 1], recv.at[d - 1], device(level, d))
                       for d in range(1, counts[level])]
        return copies

    def spread(step):
        copies = []
        for group, order in enumerate(orders):
            level, (_, at, m) = order[step], spots[group][step]
            _, (_, _, send, recv) = links(group, step)
            block = out.at[pl.ds(at, m)]
            copies += [copy(block, block, send.at[d - 1], recv.at[d - 1], device(level, d))
                       for d in range(1, counts[level])]
        return copies

    def fold(step):
        arrive(scatter(step))
        for group, order in enumerate(orders):
            _, at, m = spots[group][step]
            land, _ = links(group, step)
            value = x[pl.ds(at, m)]
            for d in range(counts[order[step]] - 1):
                value += land[d]
            if step == 2:
                out[pl.ds(at, m)] = value
            else:
                x[pl.ds(at, m)] = value

    def begin(copies):
        for sent in copies:
            sent.start()

    def arrive(copies):
        for sent in copies:
            sent.wait_recv()

    pl.semaphore_wait(barrier, sum(counts) - 3)
    begin(scatter(0))
    fold(0)
    begin(scatter(1))

    def stage(i):
        if i == 0:
            fold(1)
            begin(scatter(2))
        elif i == 1:
            fold(2)
            begin(spread(2))
        elif i == 2:
            arrive(spread(2))
            begin(spread(1))
        else:
            arrive(spread(1))
            begin(spread(0))

    blocks = padded // BLOCK

    def one(k, carry):
        at = pl.multiple_of(k * BLOCK, BLOCK)
        inverse = eliminate(held[pl.ds(at, BLOCK), pl.ds(at, BLOCK)])
        strip = jnp.dot(inverse, held[pl.ds(at, BLOCK), :], precision=HIGHEST, preferred_element_type=jnp.float32)
        held[pl.ds(at, BLOCK), :] = strip

        def trail(i, inner_carry):
            low = pl.multiple_of(i * BLOCK, BLOCK)
            side = held[pl.ds(at, BLOCK), pl.ds(low, BLOCK)]
            held[pl.ds(low, BLOCK), :] -= jnp.dot(
                side.T, held[pl.ds(at, BLOCK), :], precision=HIGHEST, preferred_element_type=jnp.float32
            )
            return inner_carry

        lax.fori_loop(k + 1, blocks, trail, 0)
        for i in range(4):
            @pl.when(k == min(i, blocks - 1))
            def _():
                stage(i)

        return carry

    lax.fori_loop(0, blocks, one, 0)
    inverse_out[...] = held[:size, padded : padded + size]
    arrive(spread(0))
    for j in range(wide):
        total[:, j * LANES : (j + 1) * LANES] = out[j * tall : (j + 1) * tall].reshape(size, LANES)
    for level in range(3):
        for sent in scatter(level) + spread(level):
            sent.wait_send()


def finish(sums, gram):
    n_row, n_col = lax.axis_size("row"), lax.axis_size("col")
    width = gram.shape[1]
    assert n_row % 2 == 0 and width % TILE == 0 and 2 * width % LANES == 0
    padded = -(-width // BLOCK) * BLOCK
    tiles = width * 2 * width // (TILE * LANES)
    devices = n_row * n_col
    units = -(-tiles // devices)
    tiles = units * devices
    less = max(1, units // 3)
    shares = ((units - less) * devices, less * devices)
    counts = [2, n_row // 2, n_col]
    dma = pltpu.SemaphoreType.DMA
    lands, sems = [], []
    for share, order in zip(shares, ((0, 1, 2), (0, 2, 1))):
        size = share
        for level in order:
            size //= counts[level]
            lands.append(pltpu.VMEM((counts[level] - 1, size, TILE, LANES), jnp.float32))
            sems += [dma((counts[level] - 1,))] * 4
    vmem = pl.BlockSpec(memory_space=pltpu.VMEM)
    return pl.pallas_call(
        functools.partial(finish_kernel, n_row, n_col, shares),
        out_shape=(jax.ShapeDtypeStruct((width, 2 * width), jnp.float32),
                   jax.ShapeDtypeStruct((width, width), jnp.float32)),
        in_specs=[vmem, vmem],
        out_specs=(vmem, vmem),
        scratch_shapes=[
            pltpu.VMEM((tiles, TILE, LANES), jnp.float32),
            pltpu.VMEM((tiles, TILE, LANES), jnp.float32),
            pltpu.VMEM((padded, 2 * padded), jnp.float32),
        ] + lands + sems,
        compiler_params=pltpu.CompilerParams(collective_id=1, has_side_effects=True),
    )(sums, gram)


def body(corner, edge, sketch):
    sums, gram = move(corner, edge, sketch.T)
    total, inverse = finish(sums, gram)
    width = gram.shape[1]
    inverse = inverse[width - RANK :]
    half = jnp.dot(inverse, total, precision=lax.Precision.HIGH)

    def turn(side):
        return lax.dot_general(side, inverse, (((1,), (1,)), ((), ())), precision=lax.Precision.HIGH)

    return turn(half[:, :width]), turn(half[:, width:])


def solution(mesh):
    placed = (P("row", "col"), P("row", "col"), P("col", None))
    return jax.shard_map(body, mesh=mesh, in_specs=placed, out_specs=(P(), P()), check_vma=False)
```

```python
import functools

import jax
import jax.numpy as jnp
from jax import lax
from jax.experimental import pallas as pl
from jax.experimental.pallas import tpu as pltpu
from jax.sharding import PartitionSpec as P

RANK = 400
HIGHEST = lax.Precision.HIGHEST
BLOCK = 128
TILE = 8
LANES = 128
SLOTS = 3
AHEAD = 2
VMEM_LIMIT = 67043328
PROMPT = 12
LATE = 6


def across(left, right):
    return lax.dot_general(left, right, (((1,), (1,)), ((), ())), preferred_element_type=jnp.float32)


def plan(part, n_row):
    sub = LANES if part % LANES == 0 else part
    pieces = part // sub
    if pieces % 5 or pieces < 25:
        return sub, pieces, 1, [pieces], pieces, [pieces - 1 + n_row], 0, 1, 0
    groups = []
    while sum(groups) + 12 < pieces:
        groups.append(6)
    left = pieces - sum(groups)
    groups += [left - left // 2 + left % 2, left // 2 - left % 2] if left > 6 else [left]
    lead = sum(groups[:2])
    lag, stride = 3, 5
    total = pieces + lag + stride * (n_row - 1) - lead
    parts = [6, 6]
    total -= 12
    for g in range(2, len(groups)):
        parts.append(total // (len(groups) - g))
        total -= parts[-1]
    return sub, pieces, 5, groups, lead, parts, lag, stride, pieces - 7


def move_kernel(n_row, n_col, shape, corner, edge, sketch, sums, gram, cols, ring, images, mine, away, near, upper, lower, rows, scratch, square, land, piece, *sems):
    (load_sem, near_send, near_recv, chain_send, upper_recv, lower_recv,
     cast_send, cast_recv, back_send, back_recv, swap_send, swap_recv,
     fold_send, fold_recv, part_send, part_recv, full_send, full_recv) = sems
    sub, pieces, tiles, groups, lead, parts, lag, stride, hold = shape
    ratio = n_col // n_row
    me_row, me_col = lax.axis_index("row"), lax.axis_index("col")
    place, half = me_col // ratio, lax.rem(me_col, ratio)
    part = cols.shape[1]
    chunk = part // tiles
    tmp = scratch if pieces > 1 else images.at[0, 0, 0]
    per_tile = pieces // tiles

    owner = place == me_row
    has_upper = jnp.logical_and(place >= me_row, place < n_row - 1)
    has_lower = jnp.logical_and(place <= me_row, place > 0)
    to_lower, to_upper = place > me_row, place < me_row
    back_up = jnp.logical_and(place >= me_row, place < n_row - 1)
    back_down = jnp.logical_and(place <= me_row, place > 0)

    def partner(d):
        return (me_row, place * ratio + lax.rem(half + d, ratio))

    def peer(d):
        return (lax.rem(me_row + d, n_row), me_col)

    def column(d):
        return (me_row, lax.rem(me_col + d, n_col))

    up_id = (me_row, lax.rem(me_col + ratio, n_col))
    down_id = (me_row, lax.rem(me_col + n_col - ratio, n_col))

    def remote(source, target, send, recv, device):
        return pltpu.make_async_remote_copy(
            src_ref=source, dst_ref=target, send_sem=send, recv_sem=recv,
            device_id=device, device_id_type=pl.DeviceIdType.MESH,
        )

    def span(s, count=1):
        if pieces == 1:
            return pl.ds(0, sub)
        return pl.ds(pl.multiple_of(s * sub, sub), count * sub)

    def near_copy(d, s):
        return remote(away.at[d - 1, :, span(s)], near.at[d - 1, :, span(s)],
                      near_send.at[d - 1, s], near_recv.at[d - 1, s], partner(d))

    def down_copy(s):
        return remote(mine.at[:, span(s)], upper.at[:, span(s)], chain_send.at[s], upper_recv.at[s], down_id)

    def up_copy(s):
        return remote(mine.at[:, span(s)], lower.at[:, span(s)], chain_send.at[s], lower_recv.at[s], up_id)

    def cast_copy(d, s):
        return remote(rows.at[0, :, span(s)], cols.at[:, span(s)], cast_send.at[d - 1, s], cast_recv.at[s], peer(d))

    def back_copy(way, s):
        return remote(rows.at[0, :, span(s)], rows.at[0, :, span(s)], back_send.at[way, s], back_recv.at[s],
                      up_id if way else down_id)

    def swap_copy(d, s):
        return remote(rows.at[0, :, span(s)], rows.at[ratio - d, :, span(s)],
                      swap_send.at[d - 1, s], swap_recv.at[ratio - d - 1, s], partner(d))

    starts = [sum(groups[:g]) for g in range(len(groups))]

    def load(matrix, t, g, slot):
        k0, width = starts[g] * sub, groups[g] * sub
        copies = []
        for pos in range(ratio):
            at = pl.multiple_of(lax.rem(half + pos, ratio) * part + t * chunk, TILE * 2)
            copies.append(pltpu.make_async_copy(
                matrix.at[pl.ds(at, chunk), k0 : k0 + width], ring.at[slot, pos, :, 0:width], load_sem.at[slot, pos]))
        return copies

    def product(left, t, g, slot):
        k0, width = starts[g] * sub, groups[g] * sub
        operand = left[:, k0 : k0 + width]
        if chunk % LANES == 0:
            block = ring[slot, :, :, 0:width].reshape(ratio * chunk, width)
            found = across(operand, block)
            return [found[:, p * chunk : (p + 1) * chunk] for p in range(ratio)]
        return [across(operand, ring[slot, p, :, 0:width]) for p in range(ratio)]

    barrier = pltpu.get_barrier_semaphore()

    def greet(device):
        pl.semaphore_signal(barrier, inc=1, device_id=device, device_id_type=pl.DeviceIdType.MESH)

    n_groups = len(groups)
    steps = [("sample", g) for g in range(n_groups)]

    def start_sample(t, g, slot):
        for copy in load(corner, t, g, slot):
            copy.start()

    def start_image(m, t, g, slot):
        for copy in load(edge if m else corner, t, g, slot):
            copy.start()

    total_sample = tiles * n_groups

    def start_at(index):
        if index < total_sample:
            start_sample(index // n_groups, index % n_groups, index % SLOTS)
        else:
            index -= total_sample
            g, rest = divmod(index, 2 * tiles)
            start_image(rest % 2, rest // 2, g, (index + total_sample) % SLOTS)

    for index in range(AHEAD):
        start_at(index)
    for d in range(1, n_row):
        greet(peer(d))
    for d in range(1, n_col):
        greet(column(d))

    def gather(s):
        total = mine[:, span(s)].astype(jnp.float32)
        for d in range(1, ratio):
            near_copy(d, s).wait_recv()
            total += near[d - 1, :, span(s)].astype(jnp.float32)
        tmp[...] = total

        @pl.when(has_upper)
        def _():
            down_copy(s).wait_recv()
            tmp[...] += upper[:, span(s)].astype(jnp.float32)

        @pl.when(has_lower)
        def _():
            up_copy(s).wait_recv()
            tmp[...] += lower[:, span(s)].astype(jnp.float32)

        @pl.when(owner)
        def _():
            value = tmp[...].astype(jnp.bfloat16)
            rows[0, :, span(s)] = value
            cols[:, span(s)] = value
            for d in range(1, n_row):
                cast_copy(d, s).start()

            @pl.when(place < n_row - 1)
            def _():
                back_copy(1, s).start()

            @pl.when(place > 0)
            def _():
                back_copy(0, s).start()

        @pl.when(to_lower)
        def _():
            mine[:, span(s)] = tmp[...].astype(jnp.bfloat16)
            down_copy(s).start()

        @pl.when(to_upper)
        def _():
            mine[:, span(s)] = tmp[...].astype(jnp.bfloat16)
            up_copy(s).start()

    prompt = PROMPT if pieces > PROMPT else pieces
    late = min(prompt + LATE, pieces)

    def hand_back(s):
        @pl.when(jnp.logical_not(owner))
        def _():
            back_copy(0, s).wait_recv()

            @pl.when(jnp.logical_and(to_lower, place < n_row - 1))
            def _():
                back_copy(1, s).start()

            @pl.when(jnp.logical_and(to_upper, place > 0))
            def _():
                back_copy(0, s).start()

    def swap(first, last):
        for s in range(first, last):
            for d in range(1, ratio):
                swap_copy(d, s).start()

    wait = lag + stride * jnp.abs(place - me_row)

    def advance(first, p):
        if first < pieces:
            @pl.when(p < pieces)
            def _():
                gather(p)

        @pl.when(jnp.logical_and(p >= wait, p < wait + pieces))
        def _():
            hand_back(p - wait)

        turn = p - jnp.maximum(wait, hold)

        @pl.when(jnp.logical_and(turn >= 0, turn < prompt))
        def _():
            for d in range(1, ratio):
                swap_copy(d, turn).start()

    def positions(first, start, stop):
        def one(p, carry):
            advance(first, p)
            return carry

        lax.fori_loop(start, stop, one, 0)

    source = jnp.where(to_lower, n_row - 1 - place, jnp.where(to_upper, place, jnp.maximum(n_row - 1 - place, place)))

    def early(t):
        return jnp.clip(2 * t - 1 - 2 * source, 0, lead) if tiles > 1 else 0

    begin = jnp.maximum(groups[0], lead - 2 * source)
    floor = max(groups[0], lead - 2 * (n_row - 1))

    def sample_tile(t, carry):
        for g in range(n_groups):
            index = t * n_groups + g
            slot = lax.rem(index, SLOTS)
            for copy in load(corner, t, g, slot):
                copy.wait()
            later = g + AHEAD
            if later < n_groups:
                start_sample(t, later, lax.rem(index + AHEAD, SLOTS))
            else:
                later_t, later_g = t + later // n_groups, later % n_groups

                @pl.when(later_t < tiles)
                def _():
                    start_sample(later_t, later_g, lax.rem(index + AHEAD, SLOTS))

            found = product(sketch, t, g, slot)
            if g > 0:
                found = [images[0, 0, p] + found[p] for p in range(ratio)]
            if g < n_groups - 1:
                for p in range(ratio):
                    images[0, 0, p] = found[p]
            else:
                at = span(t * per_tile, per_tile)
                mine[:, at] = found[0].astype(jnp.bfloat16)
                for d in range(1, ratio):
                    away[d - 1, :, at] = found[d].astype(jnp.bfloat16)

        @pl.when(t == 0)
        def _():
            pl.semaphore_wait(barrier, n_row + n_col - 2)

        for d in range(1, ratio):
            for i in range(per_tile):
                near_copy(d, t * per_tile + i).start()
        if tiles > 1:
            positions(0, early(t - 1), early(t))
        return carry

    lax.fori_loop(0, tiles, sample_tile, 0)
    for index in range(AHEAD):
        start_at(total_sample + index)
    positions(0, early(tiles - 1), begin)

    width, padded = cols.shape[0], square.shape[0]
    big = padded // n_row
    small = big // n_col

    def at_rows(index, size):
        return pl.ds(pl.multiple_of(index, TILE), size)

    folds, pieces_out, fulls = [], [], []

    def start_gram():
        square[0:width, :] = across(cols[...], cols[...])
        if padded > width:
            square[width:padded, :] = jnp.zeros((padded - width, width), jnp.float32)
        for d in range(1, n_col):
            chunk_at = me_row * big + lax.rem(me_col + d, n_col) * small
            folds.append(remote(square.at[at_rows(chunk_at, small), :], land.at[d - 1],
                                fold_send.at[d - 1], fold_recv.at[d - 1], column(d)))
            folds[-1].start()
        swap(prompt, late)

    first = 0
    for g in range(n_groups):
        for i in range(groups[g]):
            s = starts[g] + i

            @pl.when(jnp.logical_not(owner))
            def _():
                cast_copy(1, s).wait_recv()

        if g == n_groups - 1:
            start_gram()
        every = parts[g] // tiles

        def image_tile(t, carry):
            for m in range(2):
                index = total_sample + (g * tiles + t) * 2 + m
                slot = lax.rem(index, SLOTS)
                for copy in load(edge if m else corner, t, g, slot):
                    copy.wait()
                ahead = t * 2 + m + AHEAD
                into = lax.rem(index + AHEAD, SLOTS)

                @pl.when(ahead < 2 * tiles)
                def _():
                    start_image(m, t + 1, g, into)

                if g + 1 < n_groups:
                    @pl.when(ahead >= 2 * tiles)
                    def _():
                        start_image(m, 0, g + 1, into)

                found = product(cols, t, g, slot)
                for p in range(ratio):
                    if g == 0:
                        images[m, t, p] = found[p]
                    else:
                        images[m, t, p] += found[p]
            for i in range(every):
                advance(floor + first, begin + first + t * every + i)
            return carry

        lax.fori_loop(0, tiles, image_tile, 0)
        tail = parts[g] - every * tiles
        if tail:
            positions(floor + first, begin + first + every * tiles, begin + first + parts[g])
        first += parts[g]

    sums[...] = jnp.zeros_like(sums)

    def left(p, t):
        images_t = jnp.concatenate([images[m, t, p] for m in range(2)], axis=0).astype(jnp.bfloat16)
        sums[...] += across(rows[p, :, span(t * per_tile, per_tile)], images_t)

    def own_tile(t, carry):
        left(0, t)
        return carry

    def other_tile(t, carry):
        for d in range(1, ratio):
            for i in range(per_tile):
                swap_copy(d, t * per_tile + i).wait_recv()
        for p in range(1, ratio):
            left(p, t)
        return carry

    lax.fori_loop(0, tiles, own_tile, 0)
    own = at_rows(me_row * big + me_col * small, small)
    summed = square[own, :]
    for d in range(1, n_col):
        folds[d - 1].wait_recv()
        summed += land[d - 1]
    piece[...] = summed
    for d in range(1, n_col):
        pieces_out.append(remote(piece, gram.at[own, :], part_send.at[d - 1], part_recv.at[d - 1], column(d)))
        pieces_out[-1].start()
    swap(late, pieces)
    gram[own, :] = summed
    first_tiles = min(3, tiles)
    lax.fori_loop(0, first_tiles, other_tile, 0)
    for d in range(1, n_col):
        pieces_out[d - 1].wait_recv()
    block = gram.at[at_rows(me_row * big, big), :]
    for d in range(1, n_row):
        fulls.append(remote(block, block, full_send.at[d - 1], full_recv.at[d - 1], peer(d)))
        fulls[-1].start()
    if first_tiles < tiles:
        lax.fori_loop(first_tiles, tiles, other_tile, 0)
    for sent in fulls:
        sent.wait_recv()
    for sent in folds + pieces_out + fulls:
        sent.wait_send()

    def finish(s, carry):
        for d in range(1, ratio):
            near_copy(d, s).wait_send()
            swap_copy(d, s).wait_send()

        @pl.when(owner)
        def _():
            for d in range(1, n_row):
                cast_copy(d, s).wait_send()

        @pl.when(jnp.logical_not(owner))
        def _():
            down_copy(s).wait_send()

        @pl.when(back_up)
        def _():
            back_copy(1, s).wait_send()

        @pl.when(back_down)
        def _():
            back_copy(0, s).wait_send()

        return carry

    lax.fori_loop(0, pieces, finish, 0)


def move(corner, edge, sketch):
    n_row, n_col = lax.axis_size("row"), lax.axis_size("col")
    height, part = corner.shape
    width = sketch.shape[0]
    ratio = n_col // n_row
    assert ratio * n_row == n_col and height == ratio * part
    shape = plan(part, n_row)
    sub, pieces, tiles, groups = shape[:4]
    chunk = part // tiles
    dma = pltpu.SemaphoreType.DMA
    half = jnp.bfloat16
    grain = n_row * n_col * TILE
    padded = -(-width // grain) * grain
    small = padded // (n_row * n_col)
    vmem = pl.BlockSpec(memory_space=pltpu.VMEM)
    hbm = pl.BlockSpec(memory_space=pl.ANY)
    return pl.pallas_call(
        functools.partial(move_kernel, n_row, n_col, shape),
        out_shape=(jax.ShapeDtypeStruct((width, 2 * width), jnp.float32),
                   jax.ShapeDtypeStruct((padded, width), jnp.float32)),
        in_specs=[hbm, hbm, vmem],
        out_specs=(vmem, vmem),
        scratch_shapes=[
            pltpu.VMEM((width, part), half),
            pltpu.VMEM((SLOTS, ratio, chunk, max(groups) * sub), half),
            pltpu.VMEM((2, tiles, ratio, width, chunk), jnp.float32),
            pltpu.VMEM((width, part), half),
            pltpu.VMEM((ratio - 1, width, part), half),
            pltpu.VMEM((ratio - 1, width, part), half),
            pltpu.VMEM((width, part), half),
            pltpu.VMEM((width, part), half),
            pltpu.VMEM((ratio, width, part), half),
            pltpu.VMEM((width, sub) if pieces > 1 else (TILE, LANES), jnp.float32),
            pltpu.VMEM((padded, width), jnp.float32),
            pltpu.VMEM((n_col - 1, small, width), jnp.float32),
            pltpu.VMEM((small, width), jnp.float32),
            dma((SLOTS, ratio)),
            dma((ratio - 1, pieces)), dma((ratio - 1, pieces)),
            dma((pieces,)), dma((pieces,)), dma((pieces,)),
            dma((n_row - 1, pieces)), dma((pieces,)),
            dma((2, pieces)), dma((pieces,)),
            dma((ratio - 1, pieces)), dma((ratio - 1, pieces)),
            dma((n_col - 1,)), dma((n_col - 1,)), dma((n_col - 1,)), dma((n_col - 1,)),
            dma((n_row - 1,)), dma((n_row - 1,)),
        ],
        compiler_params=pltpu.CompilerParams(
            collective_id=2, has_side_effects=True, vmem_limit_bytes=VMEM_LIMIT),
    )(corner, edge, sketch)


def eliminate(block):
    size = block.shape[0]
    count = size // TILE
    lane = lax.broadcasted_iota(jnp.int32, (TILE, BLOCK), 1)
    line = lax.broadcasted_iota(jnp.int32, (2 * TILE, BLOCK), 0)
    work = [block[t * TILE : (t + 1) * TILE, :] for t in range(count)]
    top = lax.broadcasted_iota(jnp.int32, (TILE, BLOCK), 0)
    other = [(lane == top + t * TILE).astype(jnp.float32) for t in range(count)]
    done = []
    for h in range(count):
        at = h * TILE
        tiles = [h, h + 1] if h + 1 < count else [h]
        high = len(tiles) * TILE
        pair = jnp.concatenate([work[t] for t in tiles], axis=0)
        held = jnp.concatenate([other[t] for t in tiles], axis=0)
        fixed = [jnp.broadcast_to(pair[:, at + k : at + k + 1], (high, BLOCK)) for k in range(TILE)]
        ids = line[:high]
        for k in range(TILE):
            scale = 1.0 / fixed[k][k : k + 1, :]
            factor = jnp.where(ids > k, fixed[k] * scale, 0.0)
            pair = pair - factor * pair[k : k + 1, :]
            held = held - factor * held[k : k + 1, :]
            for j in range(k + 1, TILE):
                fixed[j] = fixed[j] - factor * fixed[j][k : k + 1, :]
        pivot = fixed[0][:TILE]
        for k in range(1, TILE):
            pivot = jnp.where(top == k, fixed[k][:TILE], pivot)
        upper, extra = pair[:TILE], held[:TILE]
        done.append(extra / jnp.sqrt(pivot))
        if h + 1 < count:
            work[h + 1], other[h + 1] = pair[TILE:], held[TILE:]
        if h + 2 < count:
            low = (h + 2) * TILE
            both = jnp.concatenate([upper / pivot, extra / pivot], axis=1)
            update = lax.dot_general(
                jnp.where(lane >= low, upper, 0.0), both, (((0,), (0,)), ((), ())),
                precision=HIGHEST, preferred_element_type=jnp.float32)
            for t in range(h + 2, count):
                work[t] = work[t] - update[t * TILE : (t + 1) * TILE, :BLOCK]
                other[t] = other[t] - update[t * TILE : (t + 1) * TILE, BLOCK:]
    return jnp.concatenate(done, axis=0)


def finish_kernel(n_row, n_col, shares, sums, gram, total, inverse_out, x, out, held, *rest):
    orders = ((0, 1, 2), (0, 2, 1))
    lands, sems = rest[:6], rest[6:]
    me_row, me_col = lax.axis_index("row"), lax.axis_index("col")
    inner, outer = lax.rem(me_row, 2), me_row // 2
    counts = [2, n_row // 2, n_col]
    mine = [inner, outer, me_col]

    def device(level, d):
        other = lax.rem(mine[level] + d, counts[level])
        return [(outer * 2 + other, me_col), (other * 2 + inner, me_col), (me_row, other)][level]

    def copy(source, target, send, recv, where):
        return pltpu.make_async_remote_copy(
            src_ref=source, dst_ref=target, send_sem=send, recv_sem=recv,
            device_id=where, device_id_type=pl.DeviceIdType.MESH,
        )

    barrier = pltpu.get_barrier_semaphore()
    for level in range(3):
        for d in range(1, counts[level]):
            pl.semaphore_signal(barrier, inc=1, device_id=device(level, d), device_id_type=pl.DeviceIdType.MESH)

    size = gram.shape[1]
    tall, wide = size // TILE, 2 * size // LANES
    for j in range(wide):
        x[j * tall : (j + 1) * tall] = sums[:, j * LANES : (j + 1) * LANES].reshape(tall, TILE, LANES)
    if x.shape[0] > tall * wide:
        x[tall * wide :] = jnp.zeros((x.shape[0] - tall * wide, TILE, LANES), jnp.float32)
    padded = held.shape[0]
    ids_r = lax.broadcasted_iota(jnp.int32, (padded, padded), 0)
    ids_c = lax.broadcasted_iota(jnp.int32, (padded, padded), 1)
    unit = (ids_r == ids_c).astype(jnp.float32)
    held[:, :padded] = unit
    held[:, padded:] = unit
    held[:size, :size] = gram[:size, :]

    spots = []
    for group, order in enumerate(orders):
        base, size_now = shares[0] * group, shares[group]
        steps = []
        for level in order:
            size_now //= counts[level]
            steps.append((base, base + mine[level] * size_now, size_now))
            base = base + mine[level] * size_now
        spots.append(steps)

    def links(group, step):
        n = 3 * group + step
        return lands[n], sems[4 * n : 4 * n + 4]

    def scatter(step):
        copies = []
        for group, order in enumerate(orders):
            level, (base, _, m) = order[step], spots[group][step]
            land, (send, recv, _, _) = links(group, step)
            copies += [copy(x.at[pl.ds(base + lax.rem(mine[level] + d, counts[level]) * m, m)],
                            land.at[d - 1], send.at[d - 1], recv.at[d - 1], device(level, d))
                       for d in range(1, counts[level])]
        return copies

    def spread(step):
        copies = []
        for group, order in enumerate(orders):
            level, (_, at, m) = order[step], spots[group][step]
            _, (_, _, send, recv) = links(group, step)
            block = out.at[pl.ds(at, m)]
            copies += [copy(block, block, send.at[d - 1], recv.at[d - 1], device(level, d))
                       for d in range(1, counts[level])]
        return copies

    def fold(step):
        arrive(scatter(step))
        for group, order in enumerate(orders):
            _, at, m = spots[group][step]
            land, _ = links(group, step)
            value = x[pl.ds(at, m)]
            for d in range(counts[order[step]] - 1):
                value += land[d]
            if step == 2:
                out[pl.ds(at, m)] = value
            else:
                x[pl.ds(at, m)] = value

    def begin(copies):
        for sent in copies:
            sent.start()

    def arrive(copies):
        for sent in copies:
            sent.wait_recv()

    pl.semaphore_wait(barrier, sum(counts) - 3)
    begin(scatter(0))
    fold(0)
    begin(scatter(1))

    def stage(i):
        if i == 0:
            fold(1)
            begin(scatter(2))
        elif i == 1:
            fold(2)
            begin(spread(2))
        elif i == 2:
            arrive(spread(2))
            begin(spread(1))
        else:
            arrive(spread(1))
            begin(spread(0))

    blocks = padded // BLOCK

    def one(k, carry):
        at = pl.multiple_of(k * BLOCK, BLOCK)
        inverse = eliminate(held[pl.ds(at, BLOCK), pl.ds(at, BLOCK)])
        strip = jnp.dot(inverse, held[pl.ds(at, BLOCK), :], precision=HIGHEST, preferred_element_type=jnp.float32)
        held[pl.ds(at, BLOCK), :] = strip

        def trail(i, inner_carry):
            low = pl.multiple_of(i * BLOCK, BLOCK)
            side = held[pl.ds(at, BLOCK), pl.ds(low, BLOCK)]
            held[pl.ds(low, BLOCK), :] -= jnp.dot(
                side.T, held[pl.ds(at, BLOCK), :], precision=HIGHEST, preferred_element_type=jnp.float32
            )
            return inner_carry

        lax.fori_loop(k + 1, blocks, trail, 0)
        for i in range(4):
            @pl.when(k == min(i, blocks - 1))
            def _():
                stage(i)

        return carry

    lax.fori_loop(0, blocks, one, 0)
    inverse_out[...] = held[:size, padded : padded + size]
    arrive(spread(0))
    for j in range(wide):
        total[:, j * LANES : (j + 1) * LANES] = out[j * tall : (j + 1) * tall].reshape(size, LANES)
    for level in range(3):
        for sent in scatter(level) + spread(level):
            sent.wait_send()


def finish(sums, gram):
    n_row, n_col = lax.axis_size("row"), lax.axis_size("col")
    width = gram.shape[1]
    assert n_row % 2 == 0 and width % TILE == 0 and 2 * width % LANES == 0
    padded = -(-width // BLOCK) * BLOCK
    tiles = width * 2 * width // (TILE * LANES)
    devices = n_row * n_col
    units = -(-tiles // devices)
    tiles = units * devices
    less = max(1, units // 3)
    shares = ((units - less) * devices, less * devices)
    counts = [2, n_row // 2, n_col]
    dma = pltpu.SemaphoreType.DMA
    lands, sems = [], []
    for share, order in zip(shares, ((0, 1, 2), (0, 2, 1))):
        size = share
        for level in order:
            size //= counts[level]
            lands.append(pltpu.VMEM((counts[level] - 1, size, TILE, LANES), jnp.float32))
            sems += [dma((counts[level] - 1,))] * 4
    vmem = pl.BlockSpec(memory_space=pltpu.VMEM)
    return pl.pallas_call(
        functools.partial(finish_kernel, n_row, n_col, shares),
        out_shape=(jax.ShapeDtypeStruct((width, 2 * width), jnp.float32),
                   jax.ShapeDtypeStruct((width, width), jnp.float32)),
        in_specs=[vmem, vmem],
        out_specs=(vmem, vmem),
        scratch_shapes=[
            pltpu.VMEM((tiles, TILE, LANES), jnp.float32),
            pltpu.VMEM((tiles, TILE, LANES), jnp.float32),
            pltpu.VMEM((padded, 2 * padded), jnp.float32),
        ] + lands + sems,
        compiler_params=pltpu.CompilerParams(collective_id=1, has_side_effects=True),
    )(sums, gram)


def body(corner, edge, sketch):
    sums, gram = move(corner, edge, sketch.T)
    total, inverse = finish(sums, gram)
    width = gram.shape[1]
    inverse = inverse[width - RANK :]
    half = jnp.dot(inverse, total, precision=lax.Precision.HIGH)

    def turn(side):
        return lax.dot_general(side, inverse, (((1,), (1,)), ((), ())), precision=lax.Precision.HIGH)

    return turn(half[:, :width]), turn(half[:, width:])


def solution(mesh):
    placed = (P("row", "col"), P("row", "col"), P("col", None))
    return jax.shard_map(body, mesh=mesh, in_specs=placed, out_specs=(P(), P()), check_vma=False)
```
